256 devices in a mesh: tx: 16 (over x_lo, z), ty: 8 (over y, core), gz: 2 (over x_hi).
Axes of the slice: x: 4 (x_hi: 2, x_lo: 2; x = x_hi * 2 + x_lo), y: 4, z: 8, core: 2. Of those that a mesh axis runs over, the one named last changes fastest.
Arguments:
- design: float32 [512, 2048, 256], P('tx', 'ty', 'gz'), may hold values from 0.05 to 0.95
- forward_edges: float32 [2, 12, 524288], P(None, None, ('tx', 'ty', 'gz')), may hold values from -6 to 6
- adjoint_edges: float32 [2, 12, 524288], P(None, None, ('tx', 'ty', 'gz')), may hold values from -6 to 6
- edge_basis: float32 [24, 12], replicated, may hold values from -1.75 to 1.75
- quad_weights: float32 [8], replicated, may hold values from 0.05 to 0.25
- slot_weights: bfloat16 [32768, 16, 128], P(('tx', 'ty', 'gz')), may hold values from 0.049804688 to 1
- slot_elements: int32 [32768, 16], P(('tx', 'ty', 'gz')), may hold values from 0 to 2047
- slot_blocks: int32 [32768, 16], P(('tx', 'ty', 'gz')), may hold values from 0 to 8191
- slot_counts: int32 [256, 128], P(('tx', 'ty', 'gz')), may hold values from 1 to 16, 1024 in all within a row
Outputs:
- projected: float32 [512, 2048, 256], P('tx', 'ty', 'gz')
- element_density: float32 [524288], P(('tx', 'ty', 'gz'))
The draws below stay inside these ranges and needn't reach their ends.
Inputs may be any that keep to these rules, and one draw needn't show every extreme that they name: `slot_counts`: in every row of each partition the counts sum to 128 * 16 // 2 and the largest equals 16.
All inputs are finite; a program needn't handle non-finite values.
Results may differ from the reference program's by a relative error of at most 0.00055.
Values may be sent and summed in bfloat16 or wider, within the bound.
A program may use at most 128 MiB of HBM per device.

```python
import math
import jax
import jax.numpy as jnp
import numpy as np
from jax import lax

VX = 32
VY = 256
VZ = 128
E_DEV = 2048
CAP = 16
QUAD = 8
EDGES = 12
RADIUS = 8
BLOCK_VOX = 128
TILES = 128
BLOCKS_DEV = 8192
NX = 512
NY = 2048
NZ = 256
ELEMS = 524288
SLOT_ROWS = 32768
N_TX = 16
N_TY = 8
N_GZ = 2
DEVICES = 256


def with_ends(drawn, rng, low, high):
    index_at = [jax.random.randint(jax.random.fold_in(rng, axis), (), 0, length) for axis, length in enumerate(drawn.shape)]
    widest = drawn.shape.index(max(drawn.shape))
    next_to = index_at[:widest] + [(index_at[widest] + 1) % drawn.shape[widest]] + index_at[widest + 1:]
    return drawn.at[tuple(index_at)].set(low).at[tuple(next_to)].set(high)


def block_scale(rng, extent, split, least, largest):
    loudness = 1.0
    for position, blocks in split:
        heights = jax.random.uniform(jax.random.fold_in(jax.random.fold_in(rng, 6), position), (blocks,), jnp.float32, least / len(split), largest / len(split))
        loudness = loudness * jnp.repeat(jnp.exp(heights), extent[position] // blocks).reshape((-1,) + (1,) * (len(extent) - 1 - position))
    return loudness


def length_profile(amount, total, reach, skew):
    portions = [(1 << 20) // math.isqrt(rank ** skew) + 1 for rank in range(2, amount + 1)]
    rest, holding = total - reach - (amount - 1), [1] * (amount - 1)
    while rest > 0:
        free = [i for i in range(amount - 1) if holding[i] < reach]
        mass, left = sum([portions[i] for i in free]), rest
        for i in free:
            more = min(reach - holding[i], max(1, left * portions[i] // mass), rest)
            holding[i] = holding[i] + more
            rest = rest - more
    return np.array([reach] + holding)


def ragged_sizes(rng, number_of, total, limit, lean):
    if number_of == 2:
        one = jax.random.randint(rng, (), max(1, total - limit), min(limit, total - 1) + 1)
        return jnp.stack([one, total - one])
    lengths = jnp.asarray(length_profile(number_of, total, limit, lean), jnp.int32)
    couples = (number_of - 1) // 2
    donor, receiver = lengths[1:1 + 2 * couples:2], lengths[2:2 + 2 * couples:2]
    margin = jnp.minimum(donor - 1, limit - receiver)
    moved = jax.random.randint(jax.random.fold_in(rng, 1), (couples,), 0, 1 << 20) % (margin + 1)
    lengths = lengths.at[1:1 + 2 * couples:2].set(donor - moved).at[2:2 + 2 * couples:2].set(receiver + moved)
    return lengths[jax.random.permutation(jax.random.fold_in(rng, 2), number_of)]


def centred(key, dims, spread, bound, shards=(), held_as=jnp.bfloat16):
    factor_of = block_scale(key, dims, shards, -0.22, 0.18) if shards else 1.0
    drawn = jax.random.normal(key, dims, jnp.float32) * spread * factor_of
    return jnp.minimum(jnp.maximum(drawn, -bound), bound).astype(held_as)


def setup_inputs(seed: int = 0) -> dict:
    key_of = jax.random.split(jax.random.key(seed), 10)
    design = jnp.clip(0.05 + 0.9 * jax.random.uniform(key_of[0], (NX, NY, NZ), jnp.float32) ** block_scale(key_of[0], (NX, NY, NZ), ((0, 16), (1, 8), (2, 2)), -0.2, 0.2), 0.05, 0.95)
    forward_edges = centred(key_of[1], (2, EDGES, ELEMS), 1.0, 6.0, ((2, 256),), jnp.float32)
    adjoint_edges = centred(key_of[2], (2, EDGES, ELEMS), 1.0, 6.0, ((2, 256),), jnp.float32)
    edge_basis = centred(key_of[3], (3 * QUAD, EDGES), EDGES ** -0.5, 1.75, (), jnp.float32)
    quad_weights = jnp.clip(jax.random.uniform(key_of[4], (QUAD,), jnp.float32, 0.05, 0.25), 0.05, 0.25)
    slot_weights = jnp.clip(0.049804688 + 0.9501953 * jax.random.uniform(key_of[5], (SLOT_ROWS, CAP, BLOCK_VOX), jnp.float32) ** block_scale(key_of[5], (SLOT_ROWS, CAP, BLOCK_VOX), ((0, 256),), -0.2, 0.2), 0.049804688, 1.0).astype(jnp.bfloat16)
    slot_elements = with_ends(jax.random.randint(key_of[6], (SLOT_ROWS, CAP), 0, E_DEV), jax.random.fold_in(key_of[6], 1), 0, E_DEV - 1).astype(jnp.int32)
    slot_blocks = with_ends(jax.random.randint(key_of[7], (SLOT_ROWS, CAP), 0, BLOCKS_DEV), jax.random.fold_in(key_of[7], 1), 0, BLOCKS_DEV - 1).astype(jnp.int32)
    slot_counts = jax.vmap(lambda own: ragged_sizes(own, TILES, TILES * CAP // 2, CAP, 2))(jax.random.split(key_of[8], DEVICES)).reshape((DEVICES, TILES)).astype(jnp.int32)
    return dict(design=design, forward_edges=forward_edges, adjoint_edges=adjoint_edges, edge_basis=edge_basis, quad_weights=quad_weights, slot_weights=slot_weights, slot_elements=slot_elements, slot_blocks=slot_blocks, slot_counts=slot_counts)


def filter_kernel(radius):
    values = [float(radius + 1 - abs(offset)) for offset in range(-radius, radius + 1)]
    total = sum(values)
    return [value / total for value in values]


def along(padded, kernel, dimension, length):
    summed = kernel[0] * lax.slice_in_dim(padded, 0, length, axis=dimension)
    for offset in range(1, len(kernel)):
        summed = summed + kernel[offset] * lax.slice_in_dim(padded, offset, offset + length, axis=dimension)
    return summed


def project(filtered):
    sharp = 8.0
    middle = 0.5
    span_total = math.tanh(sharp * middle) + math.tanh(sharp * (1.0 - middle))
    return (math.tanh(sharp * middle) + jnp.tanh(sharp * (filtered - middle))) / span_total


def sensitivity(edge_basis, quad_weights, forward_edges, adjoint_edges):
    highest = lax.Precision.HIGHEST
    forward_field = jnp.einsum("qk,rke->rqe", edge_basis, forward_edges, precision=highest)
    adjoint_field = jnp.einsum("qk,rke->rqe", edge_basis, adjoint_edges, precision=highest)
    product = forward_field[0] * adjoint_field[0] - forward_field[1] * adjoint_field[1]
    points = quad_weights.shape[0]
    product = product.reshape(3, points, -1).sum(axis=0)
    return jnp.dot(quad_weights, product, precision=highest)


def reference(design, forward_edges, adjoint_edges, edge_basis, quad_weights, slot_weights, slot_elements, slot_blocks, slot_counts):
    device_count = N_TX * N_TY * N_GZ
    tile_count = N_TX * N_TY
    sensitivities = sensitivity(edge_basis, quad_weights, forward_edges, adjoint_edges)
    live_slots = jnp.arange(CAP, dtype=jnp.int32)[None, None, :] < slot_counts[:, :, None]
    owner_index = jnp.arange(device_count, dtype=jnp.int32)[:, None, None]
    elements = slot_elements.reshape(device_count, tile_count, CAP) + owner_index * E_DEV
    slot_value = jnp.where(live_slots, sensitivities[elements], jnp.float32(0.0)).astype(jnp.bfloat16)
    target = jnp.arange(tile_count, dtype=jnp.int32)[None, :, None]
    block_index = (target * N_GZ + owner_index % N_GZ) * BLOCKS_DEV + slot_blocks.reshape(device_count, tile_count, CAP)
    weights = slot_weights.astype(jnp.float32).reshape(device_count, tile_count, CAP, BLOCK_VOX)
    deposits = weights * slot_value.astype(jnp.float32)[..., None]
    gradient_blocks = jnp.zeros((tile_count * N_GZ * BLOCKS_DEV, BLOCK_VOX), jnp.float32)
    gradient_blocks = gradient_blocks.at[block_index.reshape(-1)].add(deposits.reshape(-1, BLOCK_VOX))
    shaped = gradient_blocks.reshape(N_TX, N_TY, N_GZ, VX, VY, VZ)
    gradient = shaped.transpose(0, 3, 1, 4, 2, 5).reshape(NX, NY, NZ)
    updated = jnp.clip(design - 0.5 * gradient, 0.0, 1.0)
    kernel = filter_kernel(RADIUS)
    padded = jnp.pad(updated, ((RADIUS, RADIUS), (0, 0), (0, 0)), mode="wrap")
    smoothed = along(padded, kernel, 0, NX)
    padded = jnp.pad(smoothed, ((0, 0), (RADIUS, RADIUS), (0, 0)), mode="wrap")
    smoothed = along(padded, kernel, 1, NY)
    padded = jnp.pad(smoothed, ((0, 0), (0, 0), (RADIUS, RADIUS)))
    smoothed = along(padded, kernel, 2, NZ)
    normaliser = along(jnp.pad(jnp.ones((NZ,), jnp.float32), (RADIUS, RADIUS)), kernel, 0, NZ)
    projected = project(smoothed / normaliser[None, None, :])
    grouped = projected.reshape(N_TX, VX, N_TY, VY, N_GZ, VZ)
    projected_blocks = grouped.transpose(0, 2, 4, 1, 3, 5).reshape(-1, BLOCK_VOX)
    picked = projected_blocks[block_index]
    ratios = jnp.sum(weights * picked, axis=-1) / jnp.sum(weights, axis=-1)
    element_density = jnp.zeros((device_count * E_DEV,), jnp.float32)
    element_density = element_density.at[elements.reshape(-1)].add(jnp.where(live_slots, ratios, jnp.float32(0.0)).reshape(-1))
    return projected, element_density
```

```python
import functools
import math

import jax
import jax.numpy as jnp
from jax import lax
from jax.experimental import pallas as pl
from jax.experimental.pallas import tpu as pltpu
from jax.sharding import PartitionSpec as P

MESH = pl.DeviceIdType.MESH
NTX, NTY = 16, 8
TILES = NTX * NTY
VX, VY, VZ = 32, 256, 128
CAP = 16
R = 8
GROUPS = 8
PER = TILES // GROUPS
F32, BF16, I32 = jnp.float32, jnp.bfloat16, jnp.int32
HIGHEST = lax.Precision.HIGHEST


def iota(shape, dim):
    return lax.broadcasted_iota(I32, shape, dim)


def cone(distance):
    return jnp.maximum(0, R + 1 - jnp.abs(distance))


def tile_device(tile):
    return (lax.div(tile, NTY), lax.rem(tile, NTY), lax.axis_index("gz"))


def repeated(block):
    return jnp.concatenate([block] * (128 // block.shape[1]), axis=1)


def wait_bytes(ref, sem):
    pltpu.make_async_copy(ref, ref, sem).wait()


def live_mask(counts):
    column = jnp.broadcast_to(counts.astype(F32), (TILES, TILES)).T
    slot = jnp.bitwise_and(iota((TILES, 128), 1), CAP - 1).astype(F32)
    return slot < column


def deposit_kernel(
    design_hbm,
    fe_ref,
    ae_ref,
    basis_ref,
    quad_ref,
    weights_ref,
    elements_ref,
    blocks_ref,
    counts_ref,
    y_out,
    rim_out,
    w_out,
    blk_out,
    design,
    acc,
    u_ref,
    z_ref,
    meta_s,
    meta_r,
    lanes_ref,
    zsend,
    zrecv,
    ysend,
    yrecv,
    xsend,
    dsem,
    wsend,
    wrecv,
    msend,
    mrecv,
    zss,
    zrs,
    yss,
    yrs,
    xss,
    xrs,
):
    tx, ty, gz = lax.axis_index("tx"), lax.axis_index("ty"), lax.axis_index("gz")
    me = tx * NTY + ty
    barrier = pltpu.get_barrier_semaphore()

    def greet(k, carry):
        pl.semaphore_signal(
            barrier, inc=1, device_id=tile_device(lax.rem(me + k, TILES)), device_id_type=MESH
        )
        return carry

    lax.fori_loop(1, TILES, greet, 0)
    pl.semaphore_signal(barrier, inc=1, device_id=(tx, ty, 1 - gz), device_id_type=MESH)
    load_design = pltpu.make_async_copy(design_hbm, design, dsem.at[0])
    load_design.start()

    basis = basis_ref[...]
    point = jnp.bitwise_and(iota(basis.shape, 0), 7)
    quad = jnp.zeros(basis.shape, F32)
    for q in range(8):
        quad = jnp.where(point == q, quad_ref[q], quad)
    pair = lax.dot_general(
        basis * quad, basis, (((0,), (0,)), ((), ())), precision=HIGHEST, preferred_element_type=F32
    )
    real = jnp.dot(pair, ae_ref[0], precision=HIGHEST, preferred_element_type=F32)
    imag = jnp.dot(pair, ae_ref[1], precision=HIGHEST, preferred_element_type=F32)
    sens = jnp.sum(fe_ref[0] * real - fe_ref[1] * imag, axis=0, keepdims=True)
    sens = sens.astype(BF16).astype(F32)

    element = repeated(elements_ref[...])
    high, low = jnp.right_shift(element, 7), jnp.bitwise_and(element, 127)
    value = jnp.zeros((TILES, 128), F32)
    for h in range(sens.shape[1] // 128):
        row = jnp.broadcast_to(sens[:, h * 128 : (h + 1) * 128], (TILES, 128))
        value = jnp.where(high == h, jnp.take_along_axis(row, low, axis=1), value)
    value = jnp.where(live_mask(counts_ref[...]), value, 0.0)
    lane = iota((TILES, 128), 1)
    offset = jnp.bitwise_and(iota((TILES, 128), 0) + (TILES - me), 7)
    message = jnp.where(
        jnp.bitwise_and(lane, 31) < CAP, value, repeated(blocks_ref[...]).astype(F32)
    )
    message = jnp.where(jnp.right_shift(lane, 5) == jnp.right_shift(offset, 1), message, 0.0)
    meta_s[:, 0, :] = message
    lanes_ref[...] = (
        (iota((16, 16, 256), 0) * 16 + iota((16, 16, 256), 1)).astype(F32).astype(BF16)
    )

    pl.semaphore_wait(barrier, TILES)

    def send_meta(k, carry):
        tile = lax.rem(me + k, TILES)
        pltpu.make_async_remote_copy(
            src_ref=meta_s.at[tile],
            dst_ref=meta_r.at[k],
            send_sem=msend.at[0],
            recv_sem=mrecv.at[0],
            device_id=tile_device(tile),
            device_id_type=MESH,
        ).start()
        return carry

    def send_weights(k, carry):
        tile = lax.rem(me + k, TILES)
        pltpu.make_async_remote_copy(
            src_ref=weights_ref.at[tile],
            dst_ref=w_out.at[k],
            send_sem=wsend.at[0],
            recv_sem=wrecv.at[lax.div(k, PER)],
            device_id=tile_device(tile),
            device_id_type=MESH,
        ).start()
        return carry

    lax.fori_loop(1, TILES, send_meta, 0)
    lax.fori_loop(1, TILES, send_weights, 0)
    w_out[0] = weights_ref[me]
    meta_r[0] = meta_s[me]
    wait_bytes(meta_r.at[pl.ds(1, TILES - 1)], mrecv.at[0])

    row_lane = jnp.bitwise_and(iota((1, 128), 1), 31) < CAP

    def slots(r):
        even = meta_r[8 * r] + meta_r[8 * r + 2] + meta_r[8 * r + 4] + meta_r[8 * r + 6]
        odd = meta_r[8 * r + 1] + meta_r[8 * r + 3] + meta_r[8 * r + 5] + meta_r[8 * r + 7]
        values = jnp.where(row_lane, even, pltpu.roll(odd, CAP, 1))
        targets = jnp.where(row_lane, pltpu.roll(even, 128 - CAP, 1), odd).astype(I32)
        return values, targets

    for g in range(GROUPS):
        va, ta = slots(2 * g)
        vb, tb = slots(2 * g + 1)
        blk_out[pl.ds(2 * g, 1), :] = ta
        blk_out[pl.ds(2 * g + 1, 1), :] = tb
        values = jnp.broadcast_to(jnp.concatenate([va, vb], axis=1), (16, 256)).astype(BF16)
        targets = jnp.concatenate([ta, tb], axis=1)
        plane = jnp.right_shift(targets, 8)
        within = jnp.bitwise_and(targets, 255).astype(F32)
        if g == 0:
            wait_bytes(w_out.at[pl.ds(1, PER - 1)], wrecv.at[0])
        else:
            wait_bytes(w_out.at[pl.ds(g * PER, PER)], wrecv.at[g])
        chunk = w_out[pl.ds(g * PER, PER)].reshape(PER * CAP, 128)

        def deposit(x, carry, g=g, chunk=chunk, plane=plane, within=within, values=values):
            here = jnp.broadcast_to(jnp.where(plane == x, within, -1.0), (16, 256)).astype(BF16)
            spread = jnp.where(lanes_ref[...] == here[None], values[None], jnp.zeros((), BF16))
            added = jnp.dot(spread.reshape(256, 256), chunk, preferred_element_type=F32)
            if g == 0:
                acc[x] = added
            else:
                acc[x] += added
            return carry

        lax.fori_loop(0, VX, deposit, 0, unroll=2)

    load_design.wait()

    def update(x, carry):
        moved = jnp.clip(design[x] - 0.5 * acc[x], 0.0, 1.0)
        u_ref[x] = (moved - 0.5).astype(BF16)
        return carry

    lax.fori_loop(0, VX, update, 0)

    rim_planes = list(range(R)) + list(range(VX - R, VX))
    inner_planes = list(range(R, VX - R))
    halves = (rim_planes, inner_planes)

    edge = jnp.where(gz == 0, VZ - R, 0)
    zi, zl = iota((128, 128), 0), iota((128, 128), 1)
    for h, planes in enumerate(halves):
        packed = jnp.zeros((VY, 128), F32)
        for j, x in enumerate(planes):
            pick = jnp.logical_and(
                jnp.right_shift(zl, 3) == j, zi == edge + jnp.bitwise_and(zl, 7)
            )
            pick = jnp.where(pick, 1.0, 0.0).astype(BF16)
            packed = packed + jnp.dot(u_ref[x], pick, preferred_element_type=F32)
        zsend[h] = packed.astype(BF16)
        pltpu.make_async_remote_copy(
            src_ref=zsend.at[h],
            dst_ref=zrecv.at[h],
            send_sem=zss.at[h],
            recv_sem=zrs.at[h],
            device_id=(tx, ty, 1 - gz),
            device_id_type=MESH,
        ).start()

    band_z = cone(zi - zl).astype(F32).astype(BF16)
    halo_at = jnp.where(gz == 0, VZ, -R) + jnp.bitwise_and(zi, 7)
    halo_z = cone(halo_at - zl).astype(F32)
    global_z = gz * VZ + iota((1, 128), 1)
    total = jnp.zeros((1, 128), I32)
    for m in range(-R, R + 1):
        at = global_z + m
        total = total + jnp.where(jnp.logical_and(at >= 0, at < 2 * VZ), R + 1 - abs(m), 0)
    scale_z = 1.0 / total.astype(F32)

    up, down = lax.rem(ty + 1, NTY), lax.rem(ty + NTY - 1, NTY)
    for h, planes in enumerate(halves):
        wait_bytes(zrecv.at[h], zrs.at[h])
        halo = zrecv[h]
        for j in range(0, 16, 2):
            pieces = []
            for i in range(2):
                mine = jnp.where(jnp.right_shift(zi, 3) == j + i, halo_z, 0.0).astype(BF16)
                both = jnp.concatenate([u_ref[planes[j + i]], halo], axis=1)
                kernel = jnp.concatenate([band_z, mine], axis=0)
                smooth = jnp.dot(both, kernel, preferred_element_type=F32) * scale_z
                z_ref[planes[j + i]] = smooth.astype(BF16)
                pieces.append(smooth)
            at = h * 8 + j // 2
            ysend[0, at] = jnp.concatenate([p[:R] for p in pieces], axis=0).astype(BF16)
            ysend[1, at] = jnp.concatenate([p[VY - R :] for p in pieces], axis=0).astype(BF16)
        for d, target in ((0, down), (1, up)):
            pltpu.make_async_remote_copy(
                src_ref=ysend.at[d, pl.ds(h * 8, 8)],
                dst_ref=yrecv.at[d, pl.ds(h * 8, 8)],
                send_sem=yss.at[2 * h + d],
                recv_sem=yrs.at[2 * h + d],
                device_id=(tx, target, gz),
                device_id_type=MESH,
            ).start()

    band_y = cone(iota((VY, VY), 0) - iota((VY, VY), 1)).astype(F32).astype(BF16)
    oi, ki = iota((32, 32), 0), iota((32, 32), 1)
    same = jnp.right_shift(oi, 3) == jnp.right_shift(ki, 3)
    o8, k8 = jnp.bitwise_and(oi, 7), jnp.bitwise_and(ki, 7)
    below = cone(o8 - (k8 - R))
    above = cone((R + k8) - o8)
    rim_y = jnp.where(same, jnp.where(oi < 16, below, above), 0).astype(F32).astype(BF16)
    scale = 1.0 / ((R + 1) * (R + 1))
    left, right = lax.rem(tx + NTX - 1, NTX), lax.rem(tx + 1, NTX)
    for h, planes in enumerate(halves):
        for d in range(2):
            half = yrecv.at[d, pl.ds(h * 8, 8)]
            wait_bytes(half, yrs.at[2 * h + d])
        for j in range(0, 16, 2):
            a, b = planes[j], planes[j + 1]
            both = jnp.concatenate([z_ref[a], z_ref[b]], axis=1)
            smooth = jnp.dot(band_y, both, preferred_element_type=F32) * scale
            at = h * 8 + j // 2
            rims = jnp.concatenate([yrecv[1, at], yrecv[0, at]], axis=0)
            extra = jnp.dot(rim_y, rims, preferred_element_type=F32) * scale
            for i, x in enumerate((a, b)):
                mine = smooth[:, 128 * i : 128 * (i + 1)]
                top = mine[:R] + extra[R * i : R * (i + 1)]
                end = mine[VY - R :] + extra[16 + R * i : 16 + R * (i + 1)]
                full = jnp.concatenate([top, mine[R : VY - R], end], axis=0)
                y_out[x] = full
                if h == 0:
                    xsend[j + i] = full.astype(BF16)
        if h == 0:
            for d, target in ((0, left), (1, right)):
                pltpu.make_async_remote_copy(
                    src_ref=xsend.at[pl.ds(d * R, R)],
                    dst_ref=rim_out.at[pl.ds((1 - d) * R, R)],
                    send_sem=xss.at[d],
                    recv_sem=xrs.at[d],
                    device_id=(target, ty, gz),
                    device_id_type=MESH,
                ).start()

    for d in range(2):
        wait_bytes(rim_out.at[pl.ds((1 - d) * R, R)], xrs.at[d])
        wait_bytes(xsend.at[pl.ds(d * R, R)], xss.at[d])
    for h in range(2):
        wait_bytes(zsend.at[h], zss.at[h])
        for d in range(2):
            wait_bytes(ysend.at[d, pl.ds(h * 8, 8)], yss.at[2 * h + d])
    wait_bytes(meta_s.at[pl.ds(1, TILES - 1)], msend.at[0])
    wait_bytes(w_out.at[pl.ds(1, TILES - 1)], wsend.at[0])


def project_kernel(blk_ref, y_ref, rim_ref, w_ref, out_hbm, ratio_out, proj, picked, sem):
    scale = 1.0 / ((R + 1) * (R + 1))
    top = math.tanh(4.0)
    rows = 32
    strips = VY // rows

    def copy_out(s):
        span = pl.ds(pl.multiple_of(s * rows, rows), rows)
        return pltpu.make_async_copy(proj.at[:, span, :], out_hbm.at[:, span, :], sem.at[0])

    def strip(s, carry):
        span = pl.ds(pl.multiple_of(s * rows, rows), rows)

        def at(i):
            if i < 0:
                return rim_ref[i + R, span, :].astype(F32)
            if i >= VX:
                return rim_ref[i - VX + R, span, :].astype(F32)
            return y_ref[i, span, :]

        total = (R + 1) * at(0)
        for m in range(1, R + 1):
            total = total + (R + 1 - m) * (at(m) + at(-m))
        slope = at(R + 1) - at(0)
        for m in range(1, R + 1):
            slope = slope + (at(m) - at(-m))
        for o in range(VX):
            proj[o, span, :] = 0.5 + (0.5 / top) * jnp.tanh((8.0 * scale) * total)
            if o < VX - 1:
                total = total + slope
                if o < VX - 2:
                    slope = slope + (at(o + R + 2) - 2.0 * at(o + 1) + at(o - R))
        copy_out(s).start()
        return carry

    lax.fori_loop(0, strips, strip, 0)

    flat = proj.reshape(VX * VY, VZ)

    def gather(i, carry):
        r = lax.div(i, 4)
        base = lax.rem(i, 4) * 32
        for j in range(32):
            row = blk_ref[r, base + j]
            picked[pl.ds(i * 32 + j, 1), :] = flat[pl.ds(row, 1), :]
        return carry

    lax.fori_loop(0, TILES * CAP // 32, gather, 0)

    ones = jnp.ones((8, 128), BF16)
    lanes = (((1,), (1,)), ((), ()))
    for r in range(TILES * CAP // 128):
        w = w_ref[pl.ds(r * 8, 8)].reshape(128, 128)
        product = w.astype(F32) * picked[pl.ds(r * 128, 128), :]
        high = product.astype(BF16)
        low = (product - high.astype(F32)).astype(BF16)
        over = lax.dot_general(ones, high, lanes, preferred_element_type=F32)
        over = over + lax.dot_general(ones, low, lanes, preferred_element_type=F32)
        under = lax.dot_general(ones, w, lanes, preferred_element_type=F32)
        ratio_out[r] = (over / under)[:1]

    wait_bytes(proj, sem.at[0])


def return_kernel(ratio_ref, elements_ref, counts_ref, out_ref, recv, ssem, rsem):
    tx, ty = lax.axis_index("tx"), lax.axis_index("ty")
    me = tx * NTY + ty
    barrier = pltpu.get_barrier_semaphore()

    def greet(k, carry):
        pl.semaphore_signal(
            barrier, inc=1, device_id=tile_device(lax.rem(me + k, TILES)), device_id_type=MESH
        )
        return carry

    lax.fori_loop(1, TILES, greet, 0)
    pl.semaphore_wait(barrier, TILES - 1)

    def send(k, carry):
        pltpu.make_async_remote_copy(
            src_ref=ratio_ref.at[lax.div(k, 8)],
            dst_ref=recv.at[me],
            send_sem=ssem.at[0],
            recv_sem=rsem.at[0],
            device_id=tile_device(lax.rem(me + TILES - k, TILES)),
            device_id_type=MESH,
        ).start()
        return carry

    lax.fori_loop(1, TILES, send, 0)
    recv[me] = ratio_ref[0]

    offset = jnp.bitwise_and(iota((TILES, 128), 0) + (TILES - me), 7)
    chosen = jnp.right_shift(iota((TILES, 128), 1), 4) == offset
    element = jnp.where(chosen, repeated(elements_ref[...]), 0)
    element = jnp.sum(element.reshape(TILES // 8, 8, 128), axis=1)
    live = jnp.logical_and(chosen, live_mask(counts_ref[...]))
    high_e, low_e = jnp.right_shift(element, 7), jnp.bitwise_and(element, 127)

    wait_bytes(recv.at[pl.ds(1, TILES - 1)], rsem.at[0])
    ratio = jnp.where(live, recv[:, 0, :], 0.0)
    ratio = jnp.sum(ratio.reshape(TILES // 8, 8, 128), axis=1)
    total = jnp.zeros((32, 128), F32)
    lanes = (((1,), (1,)), ((), ()))
    for r in range(16):
        value = ratio[r : r + 1]
        high = value.astype(BF16).astype(F32)
        spread = jnp.where(iota((16, 128), 0) == high_e[r : r + 1], 1.0, 0.0)
        left = jnp.concatenate([spread * high, spread * (value - high)], axis=0).astype(BF16)
        right = jnp.where(iota((128, 128), 0) == low_e[r : r + 1], 1.0, 0.0).astype(BF16)
        total = total + lax.dot_general(left, right, lanes, preferred_element_type=F32)
    out_ref[...] = total[:16] + total[16:]
    wait_bytes(recv.at[pl.ds(1, TILES - 1)], ssem.at[0])


VMEM = pl.BlockSpec(memory_space=pltpu.VMEM)
SMEM = pl.BlockSpec(memory_space=pltpu.SMEM)
ANY = pl.BlockSpec(memory_space=pl.ANY)
DMA = pltpu.SemaphoreType.DMA
LIMIT = 60 << 20


def body(
    design,
    forward_edges,
    adjoint_edges,
    edge_basis,
    quad_weights,
    slot_weights,
    slot_elements,
    slot_blocks,
    slot_counts,
):
    shape = jax.ShapeDtypeStruct
    smooth, rims, weights, blocks = pl.pallas_call(
        deposit_kernel,
        name="deposit_and_smooth",
        out_shape=(
            shape((VX, VY, VZ), F32),
            shape((2 * R, VY, VZ), BF16),
            shape((TILES, CAP, 128), BF16),
            shape((TILES * CAP // 128, 128), I32),
        ),
        in_specs=[ANY, VMEM, VMEM, VMEM, SMEM, VMEM, VMEM, VMEM, VMEM],
        out_specs=(VMEM, VMEM, VMEM, VMEM),
        scratch_shapes=[
            pltpu.VMEM((VX, VY, VZ), F32),
            pltpu.VMEM((VX, VY, VZ), F32),
            pltpu.VMEM((VX, VY, VZ), BF16),
            pltpu.VMEM((VX, VY, VZ), BF16),
            pltpu.VMEM((TILES, 1, 128), F32),
            pltpu.VMEM((TILES, 1, 128), F32),
            pltpu.VMEM((16, 16, 256), BF16),
            pltpu.VMEM((2, VY, 128), BF16),
            pltpu.VMEM((2, VY, 128), BF16),
            pltpu.VMEM((2, 16, 16, 128), BF16),
            pltpu.VMEM((2, 16, 16, 128), BF16),
            pltpu.VMEM((2 * R, VY, VZ), BF16),
            DMA((1,)),
            DMA((1,)),
            DMA((GROUPS,)),
            DMA((1,)),
            DMA((1,)),
            DMA((2,)),
            DMA((2,)),
            DMA((4,)),
            DMA((4,)),
            DMA((2,)),
            DMA((2,)),
        ],
        compiler_params=pltpu.CompilerParams(
            collective_id=1, has_side_effects=True, vmem_limit_bytes=LIMIT
        ),
    )(
        design,
        forward_edges,
        adjoint_edges,
        edge_basis,
        quad_weights,
        slot_weights,
        slot_elements,
        slot_blocks,
        slot_counts,
    )
    projected, ratios = pl.pallas_call(
        project_kernel,
        name="smooth_x_and_project",
        out_shape=(
            shape((VX, VY, VZ), F32),
            shape((TILES * CAP // 128, 1, 128), F32),
        ),
        in_specs=[SMEM, VMEM, VMEM, VMEM],
        out_specs=(ANY, VMEM),
        scratch_shapes=[
            pltpu.VMEM((VX, VY, VZ), F32),
            pltpu.VMEM((TILES * CAP, 128), F32),
            DMA((1,)),
        ],
        compiler_params=pltpu.CompilerParams(vmem_limit_bytes=LIMIT),
    )(blocks, smooth, rims, weights)
    density = pl.pallas_call(
        return_kernel,
        name="return_ratios",
        out_shape=shape((16, 128), F32),
        in_specs=[VMEM, VMEM, VMEM],
        out_specs=VMEM,
        scratch_shapes=[pltpu.VMEM((TILES, 1, 128), F32), DMA((1,)), DMA((1,))],
        compiler_params=pltpu.CompilerParams(
            collective_id=2, has_side_effects=True, vmem_limit_bytes=LIMIT
        ),
    )(ratios, slot_elements, slot_counts)
    return projected, density.reshape(-1)


def solution(mesh):
    in_specs = (
        P("tx", "ty", "gz"),
        P(None, None, ("tx", "ty", "gz")),
        P(None, None, ("tx", "ty", "gz")),
        P(),
        P(),
        P(("tx", "ty", "gz"), None, None),
        P(("tx", "ty", "gz"), None),
        P(("tx", "ty", "gz"), None),
        P(("tx", "ty", "gz"), None),
    )
    out_specs = (P("tx", "ty", "gz"), P(("tx", "ty", "gz")))
    return jax.shard_map(body, mesh=mesh, in_specs=in_specs, out_specs=out_specs, check_vma=False)
```

```python
import math

import jax
import jax.numpy as jnp
from jax import lax
from jax.experimental import pallas as pl
from jax.experimental.pallas import tpu as pltpu
from jax.sharding import PartitionSpec as P

MESH = pl.DeviceIdType.MESH
NTX, NTY = 16, 8
TILES = NTX * NTY
VX, VY, VZ = 32, 256, 128
CAP = 16
R = 8
PER = 16
PIECES = 8
BATCHES = ((0, 4), (4, 2), (6, 2))
F32, BF16, I32 = jnp.float32, jnp.bfloat16, jnp.int32
HIGHEST = lax.Precision.HIGHEST


def iota(shape, dim):
    return lax.broadcasted_iota(I32, shape, dim)


def cone(distance):
    return jnp.maximum(0, R + 1 - jnp.abs(distance))


def tile_device(tile):
    return (lax.div(tile, NTY), lax.rem(tile, NTY), lax.axis_index("gz"))


def wait_bytes(ref, sem):
    pltpu.make_async_copy(ref, ref, sem).wait()


def live_mask(counts):
    return iota((CAP, TILES), 0) < counts


def step_kernel(
    design_hbm,
    fe_ref,
    ae_ref,
    basis_ref,
    quad_ref,
    weights_ref,
    elements_ref,
    blocks_ref,
    counts_ref,
    out_hbm,
    density_ref,
    design,
    acc,
    u_ref,
    z_ref,
    zx_ref,
    xrecv,
    y_ref,
    rim_ref,
    proj,
    picked,
    w_recv,
    meta_s,
    meta_r,
    lanes_ref,
    spread_ref,
    column_ref,
    blk_v,
    blk_s,
    ratios,
    returned,
    ysend,
    yrecv,
    yxrecv,
    packs,
    high_ref,
    low_ref,
    zsend,
    zrecv,
    zxrecv,
    esend,
    erecv,
    dsem,
    wsend,
    wrecv,
    msend,
    mrecv,
    hsend,
    hrecv,
    osem,
    bsem,
    rsend,
    rrecv,
):
    tx, ty, gz = lax.axis_index("tx"), lax.axis_index("ty"), lax.axis_index("gz")
    me = tx * NTY + ty
    barrier = pltpu.get_barrier_semaphore()

    def neighbour(dx, dy, dz):
        return (
            lax.rem(tx + (NTX + dx), NTX),
            lax.rem(ty + (NTY + dy), NTY),
            1 - gz if dz else gz,
        )

    def greet(k, carry):
        pl.semaphore_signal(
            barrier, inc=1, device_id=tile_device(lax.rem(me + k, TILES)), device_id_type=MESH
        )
        return carry

    lax.fori_loop(1, TILES, greet, 0)
    for dx in (-1, 0, 1):
        for dy in (-1, 0, 1):
            pl.semaphore_signal(
                barrier, inc=1, device_id=neighbour(dx, dy, 1), device_id_type=MESH
            )
    load_design = pltpu.make_async_copy(design_hbm, design, dsem.at[0])
    load_design.start()

    basis = basis_ref[...]
    point = jnp.bitwise_and(iota(basis.shape, 1), 7)
    quad = jnp.zeros(basis.shape, F32)
    for q in range(8):
        quad = jnp.where(point == q, quad_ref[q], quad)
    pair = lax.dot_general(
        basis * quad, basis, (((1,), (1,)), ((), ())), precision=HIGHEST, preferred_element_type=F32
    )
    real = jnp.dot(pair, ae_ref[:, 0, :], precision=HIGHEST, preferred_element_type=F32)
    imag = jnp.dot(pair, ae_ref[:, 1, :], precision=HIGHEST, preferred_element_type=F32)
    sens = jnp.sum(fe_ref[:, 0, :] * real - fe_ref[:, 1, :] * imag, axis=0, keepdims=True)
    sens = sens.astype(BF16).astype(F32)

    element = elements_ref[...]
    high, low = jnp.right_shift(element, 7), jnp.bitwise_and(element, 127)
    value = jnp.zeros((CAP, TILES), F32)
    for h in range(sens.shape[1] // 128):
        row = jnp.broadcast_to(sens[:, h * 128 : (h + 1) * 128], (CAP, TILES))
        value = jnp.where(high == h, jnp.take_along_axis(row, low, axis=1), value)
    value = jnp.where(live_mask(counts_ref[...]), value, 0.0)
    message = jnp.concatenate([value, blocks_ref[...].astype(F32)] * 4, axis=0)
    offset = jnp.bitwise_and(iota((128, TILES), 1) + (TILES - me), 7)
    chosen = jnp.right_shift(iota((128, TILES), 0), 5) == jnp.right_shift(offset, 1)
    meta_s[:, 0, :] = jnp.where(chosen, message, 0.0).T
    packs[...] = jnp.zeros(packs.shape, F32)
    for r in range(CAP):
        high_ref[:, 128 * r : 128 * (r + 1)] = jnp.where(
            iota((16, 128), 0) == high[r : r + 1], 1.0, 0.0
        )
        low_ref[:, 128 * r : 128 * (r + 1)] = jnp.where(
            iota((128, 128), 0) == low[r : r + 1], 1.0, 0.0
        ).astype(BF16)
    lanes_ref[...] = (
        (iota((16, 16, 256), 0) * 16 + iota((16, 16, 256), 1)).astype(F32).astype(BF16)
    )

    pl.semaphore_wait(barrier, TILES - 1 + 9)

    def sender(group):
        def send(k, carry):
            tile = lax.rem(me + k, TILES)
            pltpu.make_async_remote_copy(
                src_ref=meta_s.at[tile],
                dst_ref=meta_r.at[k],
                send_sem=msend.at[0],
                recv_sem=mrecv.at[group],
                device_id=tile_device(tile),
                device_id_type=MESH,
            ).start()
            pltpu.make_async_remote_copy(
                src_ref=weights_ref.at[tile],
                dst_ref=w_recv.at[k],
                send_sem=wsend.at[0],
                recv_sem=wrecv.at[group],
                device_id=tile_device(tile),
                device_id_type=MESH,
            ).start()
            return carry

        return send

    for group, (chunk, count) in enumerate(BATCHES):
        lax.fori_loop(max(1, chunk * PER), (chunk + count) * PER, sender(group), 0)
    w_recv[0] = weights_ref[me]
    meta_r[0] = meta_s[me]

    row_lane = jnp.bitwise_and(iota((1, 128), 1), 31) < CAP

    def slots(r):
        even = meta_r[8 * r] + meta_r[8 * r + 2] + meta_r[8 * r + 4] + meta_r[8 * r + 6]
        odd = meta_r[8 * r + 1] + meta_r[8 * r + 3] + meta_r[8 * r + 5] + meta_r[8 * r + 7]
        values = jnp.where(row_lane, even, pltpu.roll(odd, CAP, 1))
        targets = jnp.where(row_lane, pltpu.roll(even, 128 - CAP, 1), odd).astype(I32)
        blk_v[pl.ds(r, 1), :] = targets
        return values, targets

    def prepare(c):
        va, ta = slots(2 * c)
        vb, tb = slots(2 * c + 1)
        values = jnp.broadcast_to(jnp.concatenate([va, vb], axis=1), (16, 256)).astype(BF16)
        targets = jnp.concatenate([ta, tb], axis=1)
        within = jnp.bitwise_and(targets, 255).astype(F32)
        within = jnp.broadcast_to(within, (16, 256)).astype(BF16)
        spread = jnp.where(lanes_ref[...] == within[None], values[None], jnp.zeros((), BF16))
        spread_ref[:, 256 * c : 256 * (c + 1)] = spread.reshape(256, 256)
        plane = jnp.right_shift(targets, 8).astype(F32)
        for i in range(2):
            wide = jnp.broadcast_to(plane[:, 128 * i : 128 * (i + 1)], (128, 128))
            column_ref[pl.ds(16 * c + 8 * i, 8)] = wide.T.astype(BF16).reshape(8, CAP, 128)

    def deposits(p, c, n):
        chunk = w_recv[pl.ds(c * PER, n * PER)]
        column = column_ref[pl.ds(c * PER, n * PER)]
        parts = []
        for i in range(2):
            here = jnp.broadcast_to(lax.convert_element_type(2 * p + i, F32), (CAP, 128))
            part = jnp.where(column == here.astype(BF16)[None], chunk, jnp.zeros((), BF16))
            parts.append(part.reshape(n * 256, 128))
        added = jnp.dot(
            spread_ref[:, 256 * c : 256 * (c + n)],
            jnp.concatenate(parts, axis=1),
            preferred_element_type=F32,
        )
        return added[:, :128], added[:, 128:]

    copies = {}

    def copy(name, src, dst, where):
        at = len(copies)
        copies[name] = pltpu.make_async_remote_copy(
            src_ref=src,
            dst_ref=dst,
            send_sem=hsend.at[at],
            recv_sem=hrecv.at[at],
            device_id=neighbour(*where),
            device_id_type=MESH,
        )

    sides = ((-1, 0, 1), (1, VX - R, 0))
    ends = ((0, -1), (1, 1))
    for dx, start, slot in sides:
        copy(("x", dx), u_ref.at[pl.ds(start, R)], xrecv.at[pl.ds(slot * R, R)], (dx, 0, 0))
        copy(("zx", dx), zrecv.at[start // R], zxrecv.at[slot], (dx, 0, 0))
    copy(("z",), zsend, zrecv, (0, 0, 1))
    for d, dy in ends:
        copy(("y", dy), ysend.at[d], yrecv.at[d], (0, dy, 0))
        copy(("zy", dy), esend.at[d], erecv.at[d, pl.ds(0, 4)], (0, dy, 1))
        for dx, start, slot in sides:
            copy(
                ("xy", dx, dy),
                ysend.at[d, pl.ds(start // 2, 4)],
                yxrecv.at[d, pl.ds(slot * 4, 4)],
                (dx, dy, 0),
            )
            copy(("zxy", dx, dy), esend.at[d, start // R], erecv.at[d, 4 + slot], (dx, dy, 1))

    last = len(BATCHES) - 1
    for group, (c, n) in enumerate(BATCHES):
        first = max(1, c * PER)
        count = (c + n) * PER - first
        wait_bytes(meta_r.at[pl.ds(first, count)], mrecv.at[group])
        for i in range(n):
            prepare(c + i)
        wait_bytes(w_recv.at[pl.ds(first, count)], wrecv.at[group])
        if group == last:
            break

        def deposit(p, carry, group=group, c=c, n=n):
            for i, mine in enumerate(deposits(p, c, n)):
                if group == 0:
                    acc[2 * p + i] = mine
                else:
                    acc[2 * p + i] += mine
            return carry

        lax.fori_loop(0, VX // 2, deposit, 0, unroll=4)

    load_blocks = pltpu.make_async_copy(blk_v, blk_s, bsem.at[0])
    load_blocks.start()
    load_design.wait()

    edge = jnp.where(gz == 0, VZ - R, 0)
    zi, zl = iota((128, 128), 0), iota((128, 128), 1)
    pick = jnp.where(zi == edge + jnp.bitwise_and(zl, 7), 1.0, 0.0).astype(BF16)
    eighth = jnp.right_shift(zl, 3)

    def update(p, carry):
        pieces = []
        n = lax.div(p, 4)
        packed = packs[n]
        for i, mine in enumerate(deposits(p, *BATCHES[last])):
            x = 2 * p + i
            moved = jnp.clip(design[x] - 0.5 * (acc[x] + mine), 0.0, 1.0) - 0.5
            pieces.append(moved)
            moved = moved.astype(BF16)
            u_ref[x] = moved
            edges = jnp.dot(moved, pick, preferred_element_type=F32)
            j = 2 * lax.rem(p, 4) + i
            packed = jnp.where(eighth == j, edges[:128], packed)
            packed = jnp.where(eighth == R + j, edges[128:], packed)
        packs[n] = packed
        ysend[0, p] = jnp.concatenate([m[:R] for m in pieces], axis=0).astype(BF16)
        ysend[1, p] = jnp.concatenate([m[VY - R :] for m in pieces], axis=0).astype(BF16)
        return carry

    lax.fori_loop(0, VX // 2, update, 0, unroll=4)
    for n in range(VX // R):
        packed = packs[n]
        zsend[n] = packed.astype(BF16)
        esend[0, n] = packed[:R]
        esend[1, n] = packed[128 - R :]
    for kind in ("z", "zy", "y", "zxy", "xy", "x"):
        for name in copies:
            if name[0] == kind:
                copies[name].start()

    halo_at = jnp.where(gz == 0, VZ, -R) + jnp.bitwise_and(zi, 7)
    kernel_z = jnp.concatenate([cone(zi - zl), cone(halo_at - zl)], axis=0)
    kernel_z = kernel_z.astype(F32).astype(BF16)
    global_z = gz * VZ + iota((1, 128), 1)
    total = jnp.zeros((1, 128), I32)
    for m in range(-R, R + 1):
        at = global_z + m
        total = total + jnp.where(jnp.logical_and(at >= 0, at < 2 * VZ), R + 1 - abs(m), 0)
    scale_z = 1.0 / total.astype(F32)
    lane_group = jnp.right_shift(iota((16, 128), 1), 3)
    group_b = lane_group.astype(F32).astype(BF16)
    half_row = iota((16, 128), 0) < R

    def smooth_z(plane, halo, j):
        tiles = halo.reshape(8, 16, 128)
        kept = [
            jnp.where(group_b[None] == h, tiles, jnp.zeros((), BF16)).reshape(128, 128)
            for h in (j, R + j)
        ]
        both = jnp.concatenate([plane, jnp.concatenate(kept, axis=0)], axis=1)
        return (jnp.dot(both, kernel_z, preferred_element_type=F32) * scale_z).astype(BF16)

    def smooth_rows(rows, edges):
        kept = []
        for part, j in edges:
            tile = jnp.concatenate([part, part], axis=0)
            wanted = jnp.where(half_row, j, j + 1)
            kept.append(jnp.where(lane_group == wanted, tile, 0.0).astype(BF16))
        both = jnp.concatenate(
            [rows.reshape(16 * len(edges), 128), jnp.concatenate(kept, axis=0)], axis=1
        )
        both = jnp.dot(both, kernel_z, preferred_element_type=F32) * scale_z
        return both.astype(BF16).reshape(len(edges), 16, 128)

    band_y = cone(iota((VY, VY), 0) - iota((VY, VY), 1)).astype(F32).astype(BF16)
    oi, ki = iota((32, 32), 0), iota((32, 32), 1)
    same = jnp.right_shift(oi, 3) == jnp.right_shift(ki, 3)
    o8, k8 = jnp.bitwise_and(oi, 7), jnp.bitwise_and(ki, 7)
    below = cone(o8 - (k8 - R))
    above = cone((R + k8) - o8)
    rim_y = jnp.where(same, jnp.where(oi < 16, below, above), 0).astype(F32).astype(BF16)
    scale = 1.0 / ((R + 1) * (R + 1))

    def smooth_y(za, zb, low, high):
        smooth = jnp.dot(band_y, jnp.concatenate([za, zb], axis=1), preferred_element_type=F32)
        rims = jnp.concatenate([low, high], axis=0)
        extra = jnp.dot(rim_y, rims, preferred_element_type=F32)
        out = []
        for i in range(2):
            mine = smooth[:, 128 * i : 128 * (i + 1)]
            top = mine[:R] + extra[R * i : R * (i + 1)]
            end = mine[VY - R :] + extra[16 + R * i : 16 + R * (i + 1)]
            out.append(jnp.concatenate([top, mine[R : VY - R], end], axis=0) * scale)
        return out

    copies[("z",)].wait_recv()
    for dx, start, slot in sides:
        copies[("zx", dx)].start()
    for x in range(VX):
        z_ref[x] = smooth_z(u_ref[x], zrecv[x // R], x % R)
    rows = []
    for d, dy in ends:
        copies[("y", dy)].wait_recv()
        copies[("zy", dy)].wait_recv()
        edges = [(erecv[d, q // 4], R * d + 2 * (q % 4)) for q in range(VX // 2)]
        rows.append(smooth_rows(yrecv[d], edges))
    for q in range(VX // 2):
        pair = smooth_y(z_ref[2 * q], z_ref[2 * q + 1], rows[1][q], rows[0][q])
        y_ref[2 * q], y_ref[2 * q + 1] = pair

    top = math.tanh(4.0)
    strip_rows = 32

    def project(begin, end):
        def strip(s, carry):
            span = pl.ds(pl.multiple_of(s * strip_rows, strip_rows), strip_rows)

            def at(i):
                if i < 0:
                    return rim_ref[i + R, span, :]
                if i >= VX:
                    return rim_ref[i - VX + R, span, :]
                return y_ref[i, span, :]

            total = (R + 1) * at(begin)
            slope = at(begin + R + 1) - at(begin)
            for m in range(1, R + 1):
                low, high = at(begin - m), at(begin + m)
                total = total + (R + 1 - m) * (high + low)
                slope = slope + (high - low)
            for o in range(begin, end):
                proj[o, span, :] = 0.5 + (0.5 / top) * jnp.tanh((8.0 * scale) * total)
                if o < end - 1:
                    total = total + slope
                    if o < end - 2:
                        slope = slope + (at(o + R + 2) - 2.0 * at(o + 1) + at(o - R))
            return carry

        lax.fori_loop(0, VY // strip_rows, strip, 0)
        span = pl.ds(begin, end - begin)
        pltpu.make_async_copy(proj.at[span], out_hbm.at[span], osem.at[0]).start()

    project(R, VX - R)

    for dx, start, slot in sides:
        copies[("x", dx)].wait_recv()
        copies[("zx", dx)].wait_recv()
    for i in range(2 * R):
        zx_ref[i] = smooth_z(xrecv[i], zxrecv[i // R], i % R)
    rows = []
    for d, dy in ends:
        for dx, start, slot in sides:
            copies[("xy", dx, dy)].wait_recv()
            copies[("zxy", dx, dy)].wait_recv()
        edges = [(erecv[d, 4 + q // 4], R * d + 2 * (q % 4)) for q in range(R)]
        rows.append(smooth_rows(yxrecv[d], edges))
    for q in range(R):
        pair = smooth_y(zx_ref[2 * q], zx_ref[2 * q + 1], rows[1][q], rows[0][q])
        rim_ref[2 * q], rim_ref[2 * q + 1] = pair
    project(0, R)
    project(VX - R, VX)

    load_blocks.wait()
    flat = proj.reshape(VX * VY, VZ)
    ones = jnp.ones((8, 128), BF16)
    lanes = (((1,), (1,)), ((), ()))

    def ratio_row(r):
        for j in range(128):
            row = jnp.bitwise_and(blk_s[r, j], VX * VY - 1)
            picked[pl.ds(j, 1), :] = flat[pl.ds(row, 1), :]
        w = w_recv[pl.ds(r * 8, 8)].reshape(128, 128)
        product = w.astype(F32) * picked[...]
        high = product.astype(BF16)
        low = (product - high.astype(F32)).astype(BF16)
        over = lax.dot_general(ones, high, lanes, preferred_element_type=F32)
        over = over + lax.dot_general(ones, low, lanes, preferred_element_type=F32)
        under = lax.dot_general(ones, w, lanes, preferred_element_type=F32)
        ratios[r] = (over / under)[:1]

    def give_back(r, first):
        for i in range(first, 8):
            pltpu.make_async_remote_copy(
                src_ref=ratios.at[r],
                dst_ref=returned.at[me],
                send_sem=rsend.at[0],
                recv_sem=rrecv.at[0],
                device_id=tile_device(lax.rem(me + TILES - 8 * r - i, TILES)),
                device_id_type=MESH,
            ).start()

    ratio_row(0)
    give_back(0, 1)
    returned[me] = ratios[0]

    def row_step(r, carry):
        ratio_row(r)
        give_back(r, 0)
        return carry

    lax.fori_loop(1, TILES // 8, row_step, 0)

    offset = jnp.bitwise_and(iota((128, TILES), 1) + (TILES - me), 7)
    chosen = jnp.right_shift(iota((128, TILES), 0), 4) == offset
    live = live_mask(counts_ref[...])
    wait_bytes(returned.at[pl.ds(1, TILES - 1)], rrecv.at[0])
    ratio = jnp.where(chosen, returned[:, 0, :].T, 0.0)
    ratio = jnp.sum(ratio.reshape(8, CAP, TILES), axis=0)
    ratio = jnp.where(live, ratio, 0.0)
    high = ratio.astype(BF16)
    low = (ratio - high.astype(F32)).astype(BF16)
    left = []
    for part in (high, low):
        part = part.astype(F32)
        rows = [jnp.broadcast_to(part[r : r + 1], (16, 128)) for r in range(CAP)]
        left.append(jnp.concatenate(rows, axis=1) * high_ref[...])
    left = jnp.concatenate(left, axis=0).astype(BF16)
    total = lax.dot_general(left, low_ref[...], lanes, preferred_element_type=F32)
    density_ref[...] = total[:16] + total[16:]

    for name in copies:
        copies[name].wait_send()
    wait_bytes(meta_s.at[pl.ds(1, TILES - 1)], msend.at[0])
    wait_bytes(w_recv.at[pl.ds(1, TILES - 1)], wsend.at[0])
    wait_bytes(returned.at[pl.ds(1, TILES - 1)], rsend.at[0])
    wait_bytes(proj, osem.at[0])


def hand_over(in_hbm, out_hbm, held, load_sem, store_sem):
    loads, stores = [], []
    for i in range(PIECES):
        span = pl.ds(i * (VX // PIECES), VX // PIECES)
        loads.append(pltpu.make_async_copy(in_hbm.at[span], held.at[span], load_sem.at[i]))
        stores.append(pltpu.make_async_copy(held.at[span], out_hbm.at[span], store_sem.at[i]))
    for load in loads:
        load.start()
    for load, store in zip(loads, stores):
        load.wait()
        store.start()
    for store in stores:
        store.wait()


VMEM = pl.BlockSpec(memory_space=pltpu.VMEM)
SMEM = pl.BlockSpec(memory_space=pltpu.SMEM)
ANY = pl.BlockSpec(memory_space=pl.ANY)
DMA = pltpu.SemaphoreType.DMA
LIMIT = 60 << 20


def body(
    design,
    forward_edges,
    adjoint_edges,
    edge_basis,
    quad_weights,
    slot_weights,
    slot_elements,
    slot_blocks,
    slot_counts,
):
    shape = jax.ShapeDtypeStruct
    projected, density = pl.pallas_call(
        step_kernel,
        name="density_step",
        out_shape=(shape((VX, VY, VZ), F32), shape((16, 128), F32)),
        in_specs=[ANY, VMEM, VMEM, VMEM, SMEM, VMEM, VMEM, VMEM, VMEM],
        out_specs=(ANY, VMEM),
        scratch_shapes=[
            pltpu.VMEM((VX, VY, VZ), F32),
            pltpu.VMEM((VX, VY, VZ), F32),
            pltpu.VMEM((VX, VY, VZ), BF16),
            pltpu.VMEM((VX, VY, VZ), BF16),
            pltpu.VMEM((2 * R, VY, VZ), BF16),
            pltpu.VMEM((2 * R, VY, VZ), BF16),
            pltpu.VMEM((VX, VY, VZ), F32),
            pltpu.VMEM((2 * R, VY, VZ), F32),
            pltpu.VMEM((VX, VY, VZ), F32),
            pltpu.VMEM((128, 128), F32),
            pltpu.VMEM((TILES, CAP, 128), BF16),
            pltpu.VMEM((TILES, 1, 128), F32),
            pltpu.VMEM((TILES, 1, 128), F32),
            pltpu.VMEM((16, 16, 256), BF16),
            pltpu.VMEM((VY, TILES * CAP), BF16),
            pltpu.VMEM((TILES, CAP, 128), BF16),
            pltpu.VMEM((16, 128), I32),
            pltpu.SMEM((16, 128), I32),
            pltpu.VMEM((TILES // 8, 1, 128), F32),
            pltpu.VMEM((TILES, 1, 128), F32),
            pltpu.VMEM((2, 16, 16, 128), BF16),
            pltpu.VMEM((2, 16, 16, 128), BF16),
            pltpu.VMEM((2, 8, 16, 128), BF16),
            pltpu.VMEM((4, 128, 128), F32),
            pltpu.VMEM((16, TILES * CAP), F32),
            pltpu.VMEM((128, TILES * CAP), BF16),
            pltpu.VMEM((4, 128, 128), BF16),
            pltpu.VMEM((4, 128, 128), BF16),
            pltpu.VMEM((2, 128, 128), BF16),
            pltpu.VMEM((2, 4, R, 128), F32),
            pltpu.VMEM((2, 6, R, 128), F32),
            DMA((1,)),
            DMA((1,)),
            DMA((len(BATCHES),)),
            DMA((1,)),
            DMA((len(BATCHES),)),
            DMA((17,)),
            DMA((17,)),
            DMA((1,)),
            DMA((1,)),
            DMA((1,)),
            DMA((1,)),
        ],
        compiler_params=pltpu.CompilerParams(
            collective_id=1, has_side_effects=True, vmem_limit_bytes=LIMIT
        ),
    )(
        design,
        forward_edges.transpose(1, 0, 2),
        adjoint_edges.transpose(1, 0, 2),
        edge_basis.T,
        quad_weights,
        slot_weights,
        slot_elements.T,
        slot_blocks.T,
        slot_counts,
    )
    projected = pl.pallas_call(
        hand_over,
        name="hand_over",
        out_shape=shape((VX, VY, VZ), F32),
        in_specs=[ANY],
        out_specs=ANY,
        scratch_shapes=[pltpu.VMEM((VX, VY, VZ), F32), DMA((PIECES,)), DMA((PIECES,))],
    )(projected)
    return projected, density.reshape(-1)


def solution(mesh):
    in_specs = (
        P("tx", "ty", "gz"),
        P(None, None, ("tx", "ty", "gz")),
        P(None, None, ("tx", "ty", "gz")),
        P(),
        P(),
        P(("tx", "ty", "gz"), None, None),
        P(("tx", "ty", "gz"), None),
        P(("tx", "ty", "gz"), None),
        P(("tx", "ty", "gz"), None),
    )
    out_specs = (P("tx", "ty", "gz"), P(("tx", "ty", "gz")))
    return jax.shard_map(body, mesh=mesh, in_specs=in_specs, out_specs=out_specs, check_vma=False)
```

```python
import math

import jax
import jax.numpy as jnp
from jax import lax
from jax.experimental import pallas as pl
from jax.experimental.pallas import tpu as pltpu
from jax.sharding import PartitionSpec as P

MESH = pl.DeviceIdType.MESH
NTX, NTY = 16, 8
TILES = NTX * NTY
VX, VY, VZ = 32, 256, 128
CAP = 16
R = 8
PER = 16
PIECES = 8
BATCHES = ((0, 4), (4, 2), (6, 2))
F32, BF16, I32 = jnp.float32, jnp.bfloat16, jnp.int32
HIGHEST = lax.Precision.HIGHEST


def iota(shape, dim):
    return lax.broadcasted_iota(I32, shape, dim)


def cone(distance):
    return jnp.maximum(0, R + 1 - jnp.abs(distance))


def tile_device(tile):
    return (lax.div(tile, NTY), lax.rem(tile, NTY), lax.axis_index("gz"))


def wait_bytes(ref, sem):
    pltpu.make_async_copy(ref, ref, sem).wait()


def live_mask(counts):
    return iota((CAP, TILES), 0) < counts


def step_kernel(
    design_hbm,
    fe_ref,
    ae_ref,
    basis_ref,
    quad_ref,
    weights_ref,
    elements_ref,
    blocks_ref,
    counts_ref,
    out_hbm,
    density_ref,
    design,
    acc,
    u_ref,
    z_ref,
    zx_ref,
    xrecv,
    y_ref,
    rim_ref,
    proj,
    picked,
    w_recv,
    meta_s,
    meta_r,
    lanes_ref,
    spread_ref,
    column_ref,
    blk_v,
    blk_s,
    ratios,
    returned,
    ysend,
    yrecv,
    yxrecv,
    packs,
    high_ref,
    low_ref,
    zsend,
    zrecv,
    zxrecv,
    esend,
    erecv,
    dsem,
    wsend,
    wrecv,
    msend,
    mrecv,
    hsend,
    hrecv,
    osem,
    bsem,
    rsend,
    rrecv,
):
    tx, ty, gz = lax.axis_index("tx"), lax.axis_index("ty"), lax.axis_index("gz")
    me = tx * NTY + ty
    barrier = pltpu.get_barrier_semaphore()

    def neighbour(dx, dy, dz):
        return (
            lax.rem(tx + (NTX + dx), NTX),
            lax.rem(ty + (NTY + dy), NTY),
            1 - gz if dz else gz,
        )

    def greet(k, carry):
        pl.semaphore_signal(
            barrier, inc=1, device_id=tile_device(lax.rem(me + k, TILES)), device_id_type=MESH
        )
        return carry

    lax.fori_loop(1, TILES, greet, 0)
    for dx in (-1, 0, 1):
        for dy in (-1, 0, 1):
            pl.semaphore_signal(
                barrier, inc=1, device_id=neighbour(dx, dy, 1), device_id_type=MESH
            )
    load_design = pltpu.make_async_copy(design_hbm, design, dsem.at[0])
    load_design.start()

    basis = basis_ref[...]
    point = jnp.bitwise_and(iota(basis.shape, 1), 7)
    quad = jnp.zeros(basis.shape, F32)
    for q in range(8):
        quad = jnp.where(point == q, quad_ref[q], quad)
    pair = lax.dot_general(
        basis * quad, basis, (((1,), (1,)), ((), ())), precision=HIGHEST, preferred_element_type=F32
    )
    real = jnp.dot(pair, ae_ref[:, 0, :], precision=HIGHEST, preferred_element_type=F32)
    imag = jnp.dot(pair, ae_ref[:, 1, :], precision=HIGHEST, preferred_element_type=F32)
    sens = jnp.sum(fe_ref[:, 0, :] * real - fe_ref[:, 1, :] * imag, axis=0, keepdims=True)
    sens = sens.astype(BF16).astype(F32)

    element = elements_ref[...]
    high, low = jnp.right_shift(element, 7), jnp.bitwise_and(element, 127)
    value = jnp.zeros((CAP, TILES), F32)
    for h in range(sens.shape[1] // 128):
        row = jnp.broadcast_to(sens[:, h * 128 : (h + 1) * 128], (CAP, TILES))
        value = jnp.where(high == h, jnp.take_along_axis(row, low, axis=1), value)
    value = jnp.where(live_mask(counts_ref[...]), value, 0.0)
    message = jnp.concatenate([value, blocks_ref[...].astype(F32)] * 4, axis=0)
    offset = jnp.bitwise_and(iota((128, TILES), 1) + (TILES - me), 7)
    chosen = jnp.right_shift(iota((128, TILES), 0), 5) == jnp.right_shift(offset, 1)
    meta_s[:, 0, :] = jnp.where(chosen, message, 0.0).T
    packs[...] = jnp.zeros(packs.shape, F32)
    for r in range(CAP):
        high_ref[:, 128 * r : 128 * (r + 1)] = jnp.where(
            iota((16, 128), 0) == high[r : r + 1], 1.0, 0.0
        )
        low_ref[:, 128 * r : 128 * (r + 1)] = jnp.where(
            iota((128, 128), 0) == low[r : r + 1], 1.0, 0.0
        ).astype(BF16)
    lanes_ref[...] = (
        (iota((16, 16, 256), 0) * 16 + iota((16, 16, 256), 1)).astype(F32).astype(BF16)
    )

    pl.semaphore_wait(barrier, TILES - 1 + 9)

    def sender(group):
        def send(k, carry):
            tile = lax.rem(me + k, TILES)
            pltpu.make_async_remote_copy(
                src_ref=meta_s.at[tile],
                dst_ref=meta_r.at[k],
                send_sem=msend.at[0],
                recv_sem=mrecv.at[group],
                device_id=tile_device(tile),
                device_id_type=MESH,
            ).start()
            pltpu.make_async_remote_copy(
                src_ref=weights_ref.at[tile],
                dst_ref=w_recv.at[k],
                send_sem=wsend.at[0],
                recv_sem=wrecv.at[group],
                device_id=tile_device(tile),
                device_id_type=MESH,
            ).start()
            return carry

        return send

    for group, (chunk, count) in enumerate(BATCHES):
        lax.fori_loop(max(1, chunk * PER), (chunk + count) * PER, sender(group), 0)
    w_recv[0] = weights_ref[me]
    meta_r[0] = meta_s[me]

    row_lane = jnp.bitwise_and(iota((1, 128), 1), 31) < CAP

    def slots(r):
        even = meta_r[8 * r] + meta_r[8 * r + 2] + meta_r[8 * r + 4] + meta_r[8 * r + 6]
        odd = meta_r[8 * r + 1] + meta_r[8 * r + 3] + meta_r[8 * r + 5] + meta_r[8 * r + 7]
        values = jnp.where(row_lane, even, pltpu.roll(odd, CAP, 1))
        targets = jnp.where(row_lane, pltpu.roll(even, 128 - CAP, 1), odd).astype(I32)
        blk_v[pl.ds(r, 1), :] = targets
        return values, targets

    def prepare(c):
        va, ta = slots(2 * c)
        vb, tb = slots(2 * c + 1)
        values = -0.5 * jnp.concatenate([va, vb], axis=1)
        values = jnp.broadcast_to(values, (16, 256)).astype(BF16)
        targets = jnp.concatenate([ta, tb], axis=1)
        within = jnp.bitwise_and(targets, 255).astype(F32)
        within = jnp.broadcast_to(within, (16, 256)).astype(BF16)
        spread = jnp.where(lanes_ref[...] == within[None], values[None], jnp.zeros((), BF16))
        spread_ref[:, 256 * c : 256 * (c + 1)] = spread.reshape(256, 256)
        plane = jnp.right_shift(targets, 8).astype(F32)
        for i in range(2):
            wide = jnp.broadcast_to(plane[:, 128 * i : 128 * (i + 1)], (128, 128))
            column_ref[pl.ds(16 * c + 8 * i, 8)] = wide.T.astype(BF16).reshape(8, CAP, 128)

    def deposits(p, c, n):
        chunk = w_recv[pl.ds(c * PER, n * PER)]
        column = column_ref[pl.ds(c * PER, n * PER)]
        parts = []
        for i in range(2):
            here = jnp.broadcast_to(lax.convert_element_type(2 * p + i, F32), (CAP, 128))
            part = jnp.where(column == here.astype(BF16)[None], chunk, jnp.zeros((), BF16))
            parts.append(part.reshape(n * 256, 128))
        added = jnp.dot(
            spread_ref[:, 256 * c : 256 * (c + n)],
            jnp.concatenate(parts, axis=1),
            preferred_element_type=F32,
        )
        return added[:, :128], added[:, 128:]

    copies = {}

    def copy(name, src, dst, where):
        at = len(copies)
        copies[name] = pltpu.make_async_remote_copy(
            src_ref=src,
            dst_ref=dst,
            send_sem=hsend.at[at],
            recv_sem=hrecv.at[at],
            device_id=neighbour(*where),
            device_id_type=MESH,
        )

    sides = ((-1, 0, 1), (1, VX - R, 0))
    ends = ((0, -1), (1, 1))
    for dx, start, slot in sides:
        copy(("x", dx), u_ref.at[pl.ds(start, R)], xrecv.at[pl.ds(slot * R, R)], (dx, 0, 0))
        copy(("zx", dx), zrecv.at[start // R], zxrecv.at[slot], (dx, 0, 0))
    copy(("z",), zsend, zrecv, (0, 0, 1))
    for d, dy in ends:
        copy(("y", dy), ysend.at[d], yrecv.at[d], (0, dy, 0))
        copy(("zy", dy), esend.at[d], erecv.at[d, pl.ds(0, 4)], (0, dy, 1))
        for dx, start, slot in sides:
            copy(
                ("xy", dx, dy),
                ysend.at[d, pl.ds(start // 2, 4)],
                yxrecv.at[d, pl.ds(slot * 4, 4)],
                (dx, dy, 0),
            )
            copy(("zxy", dx, dy), esend.at[d, start // R], erecv.at[d, 4 + slot], (dx, dy, 1))

    load_design.wait()
    last = len(BATCHES) - 1
    for group, (c, n) in enumerate(BATCHES):
        first = max(1, c * PER)
        count = (c + n) * PER - first
        wait_bytes(meta_r.at[pl.ds(first, count)], mrecv.at[group])
        for i in range(n):
            prepare(c + i)
        wait_bytes(w_recv.at[pl.ds(first, count)], wrecv.at[group])
        if group == last:
            break

        def deposit(p, carry, group=group, c=c, n=n):
            for i, mine in enumerate(deposits(p, c, n)):
                if group == 0:
                    acc[2 * p + i] = design[2 * p + i] + mine
                else:
                    acc[2 * p + i] += mine
            return carry

        lax.fori_loop(0, VX // 2, deposit, 0, unroll=4)

    load_blocks = pltpu.make_async_copy(blk_v, blk_s, bsem.at[0])
    load_blocks.start()

    edge = jnp.where(gz == 0, VZ - R, 0)
    zi, zl = iota((128, 128), 0), iota((128, 128), 1)
    pick = jnp.where(zi == edge + jnp.bitwise_and(zl, 7), 1.0, 0.0).astype(BF16)
    eighth = jnp.right_shift(zl, 3)

    def update(p, carry):
        pieces = []
        n = lax.div(p, 4)
        packed = packs[n]
        for i, mine in enumerate(deposits(p, *BATCHES[last])):
            x = 2 * p + i
            moved = jnp.clip(acc[x] + mine, 0.0, 1.0) - 0.5
            pieces.append(moved)
            moved = moved.astype(BF16)
            u_ref[x] = moved
            edges = jnp.dot(moved, pick, preferred_element_type=F32)
            j = 2 * lax.rem(p, 4) + i
            packed = jnp.where(eighth == j, edges[:128], packed)
            packed = jnp.where(eighth == R + j, edges[128:], packed)
        packs[n] = packed
        ysend[0, p] = jnp.concatenate([m[:R] for m in pieces], axis=0).astype(BF16)
        ysend[1, p] = jnp.concatenate([m[VY - R :] for m in pieces], axis=0).astype(BF16)
        return carry

    lax.fori_loop(0, VX // 2, update, 0, unroll=4)
    for n in range(VX // R):
        packed = packs[n]
        zsend[n] = packed.astype(BF16)
        esend[0, n] = packed[:R]
        esend[1, n] = packed[128 - R :]
    for kind in ("z", "zy", "y", "zxy", "xy", "x"):
        for name in copies:
            if name[0] == kind:
                copies[name].start()

    halo_at = jnp.where(gz == 0, VZ, -R) + jnp.bitwise_and(zi, 7)
    kernel_z = jnp.concatenate([cone(zi - zl), cone(halo_at - zl)], axis=0)
    kernel_z = kernel_z.astype(F32).astype(BF16)
    global_z = gz * VZ + iota((1, 128), 1)
    total = jnp.zeros((1, 128), I32)
    for m in range(-R, R + 1):
        at = global_z + m
        total = total + jnp.where(jnp.logical_and(at >= 0, at < 2 * VZ), R + 1 - abs(m), 0)
    scale_z = 1.0 / total.astype(F32)
    lane_group = jnp.right_shift(iota((16, 128), 1), 3)
    group_b = lane_group.astype(F32).astype(BF16)
    half_row = iota((16, 128), 0) < R

    def smooth_z(plane, halo, j):
        tiles = halo.reshape(8, 16, 128)
        kept = [
            jnp.where(group_b[None] == h, tiles, jnp.zeros((), BF16)).reshape(128, 128)
            for h in (j, R + j)
        ]
        both = jnp.concatenate([plane, jnp.concatenate(kept, axis=0)], axis=1)
        return (jnp.dot(both, kernel_z, preferred_element_type=F32) * scale_z).astype(BF16)

    def smooth_rows(rows, edges):
        kept = []
        for part, j in edges:
            tile = jnp.concatenate([part, part], axis=0)
            wanted = jnp.where(half_row, j, j + 1)
            kept.append(jnp.where(lane_group == wanted, tile, 0.0).astype(BF16))
        both = jnp.concatenate(
            [rows.reshape(16 * len(edges), 128), jnp.concatenate(kept, axis=0)], axis=1
        )
        both = jnp.dot(both, kernel_z, preferred_element_type=F32) * scale_z
        return both.astype(BF16).reshape(len(edges), 16, 128)

    band_y = cone(iota((VY, VY), 0) - iota((VY, VY), 1)).astype(F32).astype(BF16)
    oi, ki = iota((32, 32), 0), iota((32, 32), 1)
    same = jnp.right_shift(oi, 3) == jnp.right_shift(ki, 3)
    o8, k8 = jnp.bitwise_and(oi, 7), jnp.bitwise_and(ki, 7)
    below = cone(o8 - (k8 - R))
    above = cone((R + k8) - o8)
    rim_y = jnp.where(same, jnp.where(oi < 16, below, above), 0).astype(F32).astype(BF16)
    scale = 1.0 / ((R + 1) * (R + 1))

    def smooth_y(za, zb, low, high):
        smooth = jnp.dot(band_y, jnp.concatenate([za, zb], axis=1), preferred_element_type=F32)
        rims = jnp.concatenate([low, high], axis=0)
        extra = jnp.dot(rim_y, rims, preferred_element_type=F32)
        out = []
        for i in range(2):
            mine = smooth[:, 128 * i : 128 * (i + 1)]
            top = mine[:R] + extra[R * i : R * (i + 1)]
            end = mine[VY - R :] + extra[16 + R * i : 16 + R * (i + 1)]
            out.append(jnp.concatenate([top, mine[R : VY - R], end], axis=0) * scale)
        return out

    copies[("z",)].wait_recv()
    for dx, start, slot in sides:
        copies[("zx", dx)].start()
    for x in range(VX):
        z_ref[x] = smooth_z(u_ref[x], zrecv[x // R], x % R)
    rows = []
    for d, dy in ends:
        copies[("y", dy)].wait_recv()
        copies[("zy", dy)].wait_recv()
        edges = [(erecv[d, q // 4], R * d + 2 * (q % 4)) for q in range(VX // 2)]
        rows.append(smooth_rows(yrecv[d], edges))
    for q in range(VX // 2):
        pair = smooth_y(z_ref[2 * q], z_ref[2 * q + 1], rows[1][q], rows[0][q])
        y_ref[2 * q], y_ref[2 * q + 1] = pair

    top = math.tanh(4.0)
    strip_rows = 32

    def project(begin, end):
        def strip(s, carry):
            span = pl.ds(pl.multiple_of(s * strip_rows, strip_rows), strip_rows)

            def at(i):
                if i < 0:
                    return rim_ref[i + R, span, :]
                if i >= VX:
                    return rim_ref[i - VX + R, span, :]
                return y_ref[i, span, :]

            total = (R + 1) * at(begin)
            slope = at(begin + R + 1) - at(begin)
            for m in range(1, R + 1):
                low, high = at(begin - m), at(begin + m)
                total = total + (R + 1 - m) * (high + low)
                slope = slope + (high - low)
            for o in range(begin, end):
                proj[o, span, :] = 0.5 + (0.5 / top) * jnp.tanh((8.0 * scale) * total)
                if o < end - 1:
                    total = total + slope
                    if o < end - 2:
                        slope = slope + (at(o + R + 2) - 2.0 * at(o + 1) + at(o - R))
            return carry

        lax.fori_loop(0, VY // strip_rows, strip, 0)
        span = pl.ds(begin, end - begin)
        pltpu.make_async_copy(proj.at[span], out_hbm.at[span], osem.at[0]).start()

    project(R, VX - R)

    for dx, start, slot in sides:
        copies[("x", dx)].wait_recv()
        copies[("zx", dx)].wait_recv()
    for i in range(2 * R):
        zx_ref[i] = smooth_z(xrecv[i], zxrecv[i // R], i % R)
    rows = []
    for d, dy in ends:
        for dx, start, slot in sides:
            copies[("xy", dx, dy)].wait_recv()
            copies[("zxy", dx, dy)].wait_recv()
        edges = [(erecv[d, 4 + q // 4], R * d + 2 * (q % 4)) for q in range(R)]
        rows.append(smooth_rows(yxrecv[d], edges))
    for q in range(R):
        pair = smooth_y(zx_ref[2 * q], zx_ref[2 * q + 1], rows[1][q], rows[0][q])
        rim_ref[2 * q], rim_ref[2 * q + 1] = pair
    project(0, R)
    project(VX - R, VX)

    load_blocks.wait()
    flat = proj.reshape(VX * VY, VZ)
    ones = jnp.ones((8, 128), BF16)
    lanes = (((1,), (1,)), ((), ()))

    def gather(r):
        base = pl.multiple_of(128 * lax.rem(r, 2), 128)
        for j in range(128):
            row = jnp.bitwise_and(blk_s[r, j], VX * VY - 1)
            picked[pl.ds(base + j, 1), :] = flat[pl.ds(row, 1), :]

    def ratio_row(r):
        base = pl.multiple_of(128 * lax.rem(r, 2), 128)
        w = w_recv[pl.ds(r * 8, 8)].reshape(128, 128)
        product = w.astype(F32) * picked[pl.ds(base, 128), :]
        high = product.astype(BF16)
        low = (product - high.astype(F32)).astype(BF16)
        over = lax.dot_general(ones, high, lanes, preferred_element_type=F32)
        over = over + lax.dot_general(ones, low, lanes, preferred_element_type=F32)
        under = lax.dot_general(ones, w, lanes, preferred_element_type=F32)
        ratios[r] = (over / under)[:1]

    def give_back(r, first):
        for i in range(first, 8):
            pltpu.make_async_remote_copy(
                src_ref=ratios.at[r],
                dst_ref=returned.at[me],
                send_sem=rsend.at[0],
                recv_sem=rrecv.at[0],
                device_id=tile_device(lax.rem(me + TILES - 8 * r - i, TILES)),
                device_id_type=MESH,
            ).start()

    def row_step(r, carry):
        give_back(r - 2, 0)
        ratio_row(r - 1)
        gather(r)
        return carry

    rows = TILES // 8
    gather(jnp.int32(0))
    ratio_row(jnp.int32(0))
    gather(jnp.int32(1))
    give_back(jnp.int32(0), 1)
    returned[me] = ratios[0]
    ratio_row(jnp.int32(1))
    gather(jnp.int32(2))
    lax.fori_loop(3, rows, row_step, 0)
    ratio_row(jnp.int32(rows - 1))
    give_back(jnp.int32(rows - 2), 0)
    give_back(jnp.int32(rows - 1), 0)

    offset = jnp.bitwise_and(iota((128, TILES), 1) + (TILES - me), 7)
    chosen = jnp.right_shift(iota((128, TILES), 0), 4) == offset
    live = live_mask(counts_ref[...])
    wait_bytes(returned.at[pl.ds(1, TILES - 1)], rrecv.at[0])
    ratio = jnp.where(chosen, returned[:, 0, :].T, 0.0)
    ratio = jnp.sum(ratio.reshape(8, CAP, TILES), axis=0)
    ratio = jnp.where(live, ratio, 0.0)
    high = ratio.astype(BF16)
    low = (ratio - high.astype(F32)).astype(BF16)
    left = []
    for part in (high, low):
        part = part.astype(F32)
        rows = [jnp.broadcast_to(part[r : r + 1], (16, 128)) for r in range(CAP)]
        left.append(jnp.concatenate(rows, axis=1) * high_ref[...])
    left = jnp.concatenate(left, axis=0).astype(BF16)
    total = lax.dot_general(left, low_ref[...], lanes, preferred_element_type=F32)
    density_ref[...] = total[:16] + total[16:]

    for name in copies:
        copies[name].wait_send()
    wait_bytes(meta_s.at[pl.ds(1, TILES - 1)], msend.at[0])
    wait_bytes(w_recv.at[pl.ds(1, TILES - 1)], wsend.at[0])
    wait_bytes(returned.at[pl.ds(1, TILES - 1)], rsend.at[0])
    wait_bytes(proj, osem.at[0])


def hand_over(in_hbm, out_hbm, held, load_sem, store_sem):
    loads, stores = [], []
    for i in range(PIECES):
        span = pl.ds(i * (VX // PIECES), VX // PIECES)
        loads.append(pltpu.make_async_copy(in_hbm.at[span], held.at[span], load_sem.at[i]))
        stores.append(pltpu.make_async_copy(held.at[span], out_hbm.at[span], store_sem.at[i]))
    for load in loads:
        load.start()
    for load, store in zip(loads, stores):
        load.wait()
        store.start()
    for store in stores:
        store.wait()


VMEM = pl.BlockSpec(memory_space=pltpu.VMEM)
SMEM = pl.BlockSpec(memory_space=pltpu.SMEM)
ANY = pl.BlockSpec(memory_space=pl.ANY)
DMA = pltpu.SemaphoreType.DMA
LIMIT = 60 << 20


def body(
    design,
    forward_edges,
    adjoint_edges,
    edge_basis,
    quad_weights,
    slot_weights,
    slot_elements,
    slot_blocks,
    slot_counts,
):
    shape = jax.ShapeDtypeStruct
    projected, density = pl.pallas_call(
        step_kernel,
        name="density_step",
        out_shape=(shape((VX, VY, VZ), F32), shape((16, 128), F32)),
        in_specs=[ANY, VMEM, VMEM, VMEM, SMEM, VMEM, VMEM, VMEM, VMEM],
        out_specs=(ANY, VMEM),
        scratch_shapes=[
            pltpu.VMEM((VX, VY, VZ), F32),
            pltpu.VMEM((VX, VY, VZ), F32),
            pltpu.VMEM((VX, VY, VZ), BF16),
            pltpu.VMEM((VX, VY, VZ), BF16),
            pltpu.VMEM((2 * R, VY, VZ), BF16),
            pltpu.VMEM((2 * R, VY, VZ), BF16),
            pltpu.VMEM((VX, VY, VZ), F32),
            pltpu.VMEM((2 * R, VY, VZ), F32),
            pltpu.VMEM((VX, VY, VZ), F32),
            pltpu.VMEM((256, 128), F32),
            pltpu.VMEM((TILES, CAP, 128), BF16),
            pltpu.VMEM((TILES, 1, 128), F32),
            pltpu.VMEM((TILES, 1, 128), F32),
            pltpu.VMEM((16, 16, 256), BF16),
            pltpu.VMEM((VY, TILES * CAP), BF16),
            pltpu.VMEM((TILES, CAP, 128), BF16),
            pltpu.VMEM((16, 128), I32),
            pltpu.SMEM((16, 128), I32),
            pltpu.VMEM((TILES // 8, 1, 128), F32),
            pltpu.VMEM((TILES, 1, 128), F32),
            pltpu.VMEM((2, 16, 16, 128), BF16),
            pltpu.VMEM((2, 16, 16, 128), BF16),
            pltpu.VMEM((2, 8, 16, 128), BF16),
            pltpu.VMEM((4, 128, 128), F32),
            pltpu.VMEM((16, TILES * CAP), F32),
            pltpu.VMEM((128, TILES * CAP), BF16),
            pltpu.VMEM((4, 128, 128), BF16),
            pltpu.VMEM((4, 128, 128), BF16),
            pltpu.VMEM((2, 128, 128), BF16),
            pltpu.VMEM((2, 4, R, 128), F32),
            pltpu.VMEM((2, 6, R, 128), F32),
            DMA((1,)),
            DMA((1,)),
            DMA((len(BATCHES),)),
            DMA((1,)),
            DMA((len(BATCHES),)),
            DMA((17,)),
            DMA((17,)),
            DMA((1,)),
            DMA((1,)),
            DMA((1,)),
            DMA((1,)),
        ],
        compiler_params=pltpu.CompilerParams(
            collective_id=1, has_side_effects=True, vmem_limit_bytes=LIMIT
        ),
    )(
        design,
        forward_edges.transpose(1, 0, 2),
        adjoint_edges.transpose(1, 0, 2),
        edge_basis.T,
        quad_weights,
        slot_weights,
        slot_elements.T,
        slot_blocks.T,
        slot_counts,
    )
    projected = pl.pallas_call(
        hand_over,
        name="hand_over",
        out_shape=shape((VX, VY, VZ), F32),
        in_specs=[ANY],
        out_specs=ANY,
        scratch_shapes=[pltpu.VMEM((VX, VY, VZ), F32), DMA((PIECES,)), DMA((PIECES,))],
    )(projected)
    return projected, density.reshape(-1)


def solution(mesh):
    in_specs = (
        P("tx", "ty", "gz"),
        P(None, None, ("tx", "ty", "gz")),
        P(None, None, ("tx", "ty", "gz")),
        P(),
        P(),
        P(("tx", "ty", "gz"), None, None),
        P(("tx", "ty", "gz"), None),
        P(("tx", "ty", "gz"), None),
        P(("tx", "ty", "gz"), None),
    )
    out_specs = (P("tx", "ty", "gz"), P(("tx", "ty", "gz")))
    return jax.shard_map(body, mesh=mesh, in_specs=in_specs, out_specs=out_specs, check_vma=False)
```

```python
import math

import jax
import jax.numpy as jnp
from jax import lax
from jax.experimental import pallas as pl
from jax.experimental.pallas import tpu as pltpu
from jax.sharding import PartitionSpec as P

MESH = pl.DeviceIdType.MESH
NTX, NTY = 16, 8
TILES = NTX * NTY
VX, VY, VZ = 32, 256, 128
CAP = 16
R = 8
PER = 16
PIECES = 8
BATCHES = ((0, 4), (4, 2), (6, 1), (7, 1))
F32, BF16, I32 = jnp.float32, jnp.bfloat16, jnp.int32
HIGHEST = lax.Precision.HIGHEST


def iota(shape, dim):
    return lax.broadcasted_iota(I32, shape, dim)


def cone(distance):
    return jnp.maximum(0, R + 1 - jnp.abs(distance))


def tile_device(tile):
    return (lax.div(tile, NTY), lax.rem(tile, NTY), lax.axis_index("gz"))


def wait_bytes(ref, sem):
    pltpu.make_async_copy(ref, ref, sem).wait()


def live_mask(counts):
    return iota((CAP, TILES), 0) < counts


def step_kernel(
    design_hbm,
    fe_ref,
    ae_ref,
    basis_ref,
    quad_ref,
    weights_ref,
    elements_ref,
    blocks_ref,
    counts_ref,
    out_hbm,
    density_ref,
    design,
    acc,
    u_ref,
    z_ref,
    zx_ref,
    xrecv,
    y_ref,
    rim_ref,
    proj,
    picked,
    w_recv,
    meta_s,
    meta_r,
    lanes_ref,
    spread_ref,
    column_ref,
    blk_v,
    blk_s,
    ratios,
    returned,
    ysend,
    yrecv,
    yxrecv,
    packs,
    high_ref,
    low_ref,
    zsend,
    zrecv,
    zxrecv,
    esend,
    erecv,
    dsem,
    wsend,
    wrecv,
    msend,
    mrecv,
    hsend,
    hrecv,
    osem,
    bsem,
    rsend,
    rrecv,
):
    tx, ty, gz = lax.axis_index("tx"), lax.axis_index("ty"), lax.axis_index("gz")
    me = tx * NTY + ty
    barrier = pltpu.get_barrier_semaphore()

    def neighbour(dx, dy, dz):
        return (
            lax.rem(tx + (NTX + dx), NTX),
            lax.rem(ty + (NTY + dy), NTY),
            1 - gz if dz else gz,
        )

    def greet(k, carry):
        pl.semaphore_signal(
            barrier, inc=1, device_id=tile_device(lax.rem(me + k, TILES)), device_id_type=MESH
        )
        return carry

    lax.fori_loop(1, TILES, greet, 0)
    for dx in (-1, 0, 1):
        for dy in (-1, 0, 1):
            pl.semaphore_signal(
                barrier, inc=1, device_id=neighbour(dx, dy, 1), device_id_type=MESH
            )
    load_design = pltpu.make_async_copy(design_hbm, design, dsem.at[0])
    load_design.start()

    basis = basis_ref[...]
    point = jnp.bitwise_and(iota(basis.shape, 1), 7)
    quad = jnp.zeros(basis.shape, F32)
    for q in range(8):
        quad = jnp.where(point == q, quad_ref[q], quad)
    pair = lax.dot_general(
        basis * quad, basis, (((1,), (1,)), ((), ())), precision=HIGHEST, preferred_element_type=F32
    )
    real = jnp.dot(pair, ae_ref[:, 0, :], precision=HIGHEST, preferred_element_type=F32)
    imag = jnp.dot(pair, ae_ref[:, 1, :], precision=HIGHEST, preferred_element_type=F32)
    sens = jnp.sum(fe_ref[:, 0, :] * real - fe_ref[:, 1, :] * imag, axis=0, keepdims=True)
    sens = sens.astype(BF16).astype(F32)

    element = elements_ref[...]
    high, low = jnp.right_shift(element, 7), jnp.bitwise_and(element, 127)
    value = jnp.zeros((CAP, TILES), F32)
    for h in range(sens.shape[1] // 128):
        row = jnp.broadcast_to(sens[:, h * 128 : (h + 1) * 128], (CAP, TILES))
        value = jnp.where(high == h, jnp.take_along_axis(row, low, axis=1), value)
    value = jnp.where(live_mask(counts_ref[...]), value, 0.0)
    message = jnp.concatenate([value, blocks_ref[...].astype(F32)] * 4, axis=0)
    offset = jnp.bitwise_and(iota((128, TILES), 1) + (TILES - me), 7)
    chosen = jnp.right_shift(iota((128, TILES), 0), 5) == jnp.right_shift(offset, 1)
    meta_s[:, 0, :] = jnp.where(chosen, message, 0.0).T
    packs[...] = jnp.zeros(packs.shape, F32)
    for r in range(CAP):
        high_ref[:, 128 * r : 128 * (r + 1)] = jnp.where(
            iota((16, 128), 0) == high[r : r + 1], 1.0, 0.0
        )
        low_ref[:, 128 * r : 128 * (r + 1)] = jnp.where(
            iota((128, 128), 0) == low[r : r + 1], 1.0, 0.0
        ).astype(BF16)
    lanes_ref[...] = (
        (iota((16, 16, 256), 0) * 16 + iota((16, 16, 256), 1)).astype(F32).astype(BF16)
    )

    pl.semaphore_wait(barrier, TILES - 1 + 9)

    def sender(group):
        def send(k, carry):
            tile = lax.rem(me + k, TILES)
            pltpu.make_async_remote_copy(
                src_ref=meta_s.at[tile],
                dst_ref=meta_r.at[k],
                send_sem=msend.at[0],
                recv_sem=mrecv.at[group],
                device_id=tile_device(tile),
                device_id_type=MESH,
            ).start()
            pltpu.make_async_remote_copy(
                src_ref=weights_ref.at[tile],
                dst_ref=w_recv.at[k],
                send_sem=wsend.at[0],
                recv_sem=wrecv.at[group],
                device_id=tile_device(tile),
                device_id_type=MESH,
            ).start()
            return carry

        return send

    for group, (chunk, count) in enumerate(BATCHES):
        lax.fori_loop(max(1, chunk * PER), (chunk + count) * PER, sender(group), 0)
    w_recv[0] = weights_ref[me]
    meta_r[0] = meta_s[me]

    row_lane = jnp.bitwise_and(iota((1, 128), 1), 31) < CAP

    def slots(r):
        even = meta_r[8 * r] + meta_r[8 * r + 2] + meta_r[8 * r + 4] + meta_r[8 * r + 6]
        odd = meta_r[8 * r + 1] + meta_r[8 * r + 3] + meta_r[8 * r + 5] + meta_r[8 * r + 7]
        values = jnp.where(row_lane, even, pltpu.roll(odd, CAP, 1))
        targets = jnp.where(row_lane, pltpu.roll(even, 128 - CAP, 1), odd).astype(I32)
        blk_v[pl.ds(r, 1), :] = targets
        return values, targets

    def prepare(c):
        va, ta = slots(2 * c)
        vb, tb = slots(2 * c + 1)
        values = -0.5 * jnp.concatenate([va, vb], axis=1)
        values = jnp.broadcast_to(values, (16, 256)).astype(BF16)
        targets = jnp.concatenate([ta, tb], axis=1)
        within = jnp.bitwise_and(targets, 255).astype(F32)
        within = jnp.broadcast_to(within, (16, 256)).astype(BF16)
        spread = jnp.where(lanes_ref[...] == within[None], values[None], jnp.zeros((), BF16))
        spread_ref[:, 256 * c : 256 * (c + 1)] = spread.reshape(256, 256)
        plane = jnp.right_shift(targets, 8).astype(F32)
        for i in range(2):
            wide = jnp.broadcast_to(plane[:, 128 * i : 128 * (i + 1)], (128, 128))
            column_ref[pl.ds(16 * c + 8 * i, 8)] = wide.T.astype(BF16).reshape(8, CAP, 128)

    def deposits(p, c, n):
        chunk = w_recv[pl.ds(c * PER, n * PER)]
        column = column_ref[pl.ds(c * PER, n * PER)]
        parts = []
        for i in range(2):
            here = jnp.broadcast_to(lax.convert_element_type(2 * p + i, F32), (CAP, 128))
            part = jnp.where(column == here.astype(BF16)[None], chunk, jnp.zeros((), BF16))
            parts.append(part.reshape(n * 256, 128))
        added = jnp.dot(
            spread_ref[:, 256 * c : 256 * (c + n)],
            jnp.concatenate(parts, axis=1),
            preferred_element_type=F32,
        )
        return added[:, :128], added[:, 128:]

    copies = {}

    def copy(name, src, dst, where):
        at = len(copies)
        copies[name] = pltpu.make_async_remote_copy(
            src_ref=src,
            dst_ref=dst,
            send_sem=hsend.at[at],
            recv_sem=hrecv.at[at],
            device_id=neighbour(*where),
            device_id_type=MESH,
        )

    sides = ((-1, 0, 1), (1, VX - R, 0))
    ends = ((0, -1), (1, 1))
    for dx, start, slot in sides:
        copy(("x", dx), u_ref.at[pl.ds(start, R)], xrecv.at[pl.ds(slot * R, R)], (dx, 0, 0))
        copy(("zx", dx), zrecv.at[start // R], zxrecv.at[slot], (dx, 0, 0))
    copy(("z",), zsend, zrecv, (0, 0, 1))
    for d, dy in ends:
        copy(("y", dy), ysend.at[d], yrecv.at[d], (0, dy, 0))
        copy(("zy", dy), esend.at[d], erecv.at[d, pl.ds(0, 4)], (0, dy, 1))
        for dx, start, slot in sides:
            copy(
                ("xy", dx, dy),
                ysend.at[d, pl.ds(start // 2, 4)],
                yxrecv.at[d, pl.ds(slot * 4, 4)],
                (dx, dy, 0),
            )
            copy(("zxy", dx, dy), esend.at[d, start // R], erecv.at[d, 4 + slot], (dx, dy, 1))

    load_design.wait()
    last = len(BATCHES) - 1
    for group, (c, n) in enumerate(BATCHES):
        first = max(1, c * PER)
        count = (c + n) * PER - first
        wait_bytes(meta_r.at[pl.ds(first, count)], mrecv.at[group])
        for i in range(n):
            prepare(c + i)
        wait_bytes(w_recv.at[pl.ds(first, count)], wrecv.at[group])
        if group == last:
            break

        def deposit(p, carry, group=group, c=c, n=n):
            for i, mine in enumerate(deposits(p, c, n)):
                if group == 0:
                    acc[2 * p + i] = design[2 * p + i] + mine
                else:
                    acc[2 * p + i] += mine
            return carry

        lax.fori_loop(0, VX // 2, deposit, 0, unroll=4)

    load_blocks = pltpu.make_async_copy(blk_v, blk_s, bsem.at[0])
    load_blocks.start()

    edge = jnp.where(gz == 0, VZ - R, 0)
    zi, zl = iota((128, 128), 0), iota((128, 128), 1)
    pick = jnp.where(zi == edge + jnp.bitwise_and(zl, 7), 1.0, 0.0).astype(BF16)
    eighth = jnp.right_shift(zl, 3)

    def update(p, carry):
        pieces = []
        n = lax.div(p, 4)
        packed = packs[n]
        for i, mine in enumerate(deposits(p, *BATCHES[last])):
            x = 2 * p + i
            moved = jnp.clip(acc[x] + mine, 0.0, 1.0) - 0.5
            pieces.append(moved)
            moved = moved.astype(BF16)
            u_ref[x] = moved
            edges = jnp.dot(moved, pick, preferred_element_type=F32)
            j = 2 * lax.rem(p, 4) + i
            packed = jnp.where(eighth == j, edges[:128], packed)
            packed = jnp.where(eighth == R + j, edges[128:], packed)
        packs[n] = packed
        ysend[0, p] = jnp.concatenate([m[:R] for m in pieces], axis=0).astype(BF16)
        ysend[1, p] = jnp.concatenate([m[VY - R :] for m in pieces], axis=0).astype(BF16)
        return carry

    lax.fori_loop(0, VX // 2, update, 0, unroll=4)
    for n in range(VX // R):
        packed = packs[n]
        zsend[n] = packed.astype(BF16)
        esend[0, n] = packed[:R]
        esend[1, n] = packed[128 - R :]
    for kind in ("z", "zy", "y", "zxy", "xy", "x"):
        for name in copies:
            if name[0] == kind:
                copies[name].start()

    halo_at = jnp.where(gz == 0, VZ, -R) + jnp.bitwise_and(zi, 7)
    kernel_z = jnp.concatenate([cone(zi - zl), cone(halo_at - zl)], axis=0)
    kernel_z = kernel_z.astype(F32).astype(BF16)
    global_z = gz * VZ + iota((1, 128), 1)
    total = jnp.zeros((1, 128), I32)
    for m in range(-R, R + 1):
        at = global_z + m
        total = total + jnp.where(jnp.logical_and(at >= 0, at < 2 * VZ), R + 1 - abs(m), 0)
    scale_z = 1.0 / total.astype(F32)
    lane_group = jnp.right_shift(iota((16, 128), 1), 3)
    group_b = lane_group.astype(F32).astype(BF16)
    half_row = iota((16, 128), 0) < R

    def smooth_z(plane, halo, j):
        tiles = halo.reshape(8, 16, 128)
        kept = [
            jnp.where(group_b[None] == h, tiles, jnp.zeros((), BF16)).reshape(128, 128)
            for h in (j, R + j)
        ]
        both = jnp.concatenate([plane, jnp.concatenate(kept, axis=0)], axis=1)
        return (jnp.dot(both, kernel_z, preferred_element_type=F32) * scale_z).astype(BF16)

    def smooth_rows(rows, edges):
        kept = []
        for part, j in edges:
            tile = jnp.concatenate([part, part], axis=0)
            wanted = jnp.where(half_row, j, j + 1)
            kept.append(jnp.where(lane_group == wanted, tile, 0.0).astype(BF16))
        both = jnp.concatenate(
            [rows.reshape(16 * len(edges), 128), jnp.concatenate(kept, axis=0)], axis=1
        )
        both = jnp.dot(both, kernel_z, preferred_element_type=F32) * scale_z
        return both.astype(BF16).reshape(len(edges), 16, 128)

    band_y = cone(iota((VY, VY), 0) - iota((VY, VY), 1)).astype(F32).astype(BF16)
    oi, ki = iota((32, 32), 0), iota((32, 32), 1)
    same = jnp.right_shift(oi, 3) == jnp.right_shift(ki, 3)
    o8, k8 = jnp.bitwise_and(oi, 7), jnp.bitwise_and(ki, 7)
    below = cone(o8 - (k8 - R))
    above = cone((R + k8) - o8)
    rim_y = jnp.where(same, jnp.where(oi < 16, below, above), 0).astype(F32).astype(BF16)
    scale = 1.0 / ((R + 1) * (R + 1))

    def smooth_y(za, zb, low, high):
        smooth = jnp.dot(band_y, jnp.concatenate([za, zb], axis=1), preferred_element_type=F32)
        rims = jnp.concatenate([low, high], axis=0)
        extra = jnp.dot(rim_y, rims, preferred_element_type=F32)
        out = []
        for i in range(2):
            mine = smooth[:, 128 * i : 128 * (i + 1)]
            top = mine[:R] + extra[R * i : R * (i + 1)]
            end = mine[VY - R :] + extra[16 + R * i : 16 + R * (i + 1)]
            out.append(jnp.concatenate([top, mine[R : VY - R], end], axis=0) * scale)
        return out

    copies[("z",)].wait_recv()
    for dx, start, slot in sides:
        copies[("zx", dx)].start()
    for x in range(VX):
        z_ref[x] = smooth_z(u_ref[x], zrecv[x // R], x % R)
    rows = []
    for d, dy in ends:
        copies[("y", dy)].wait_recv()
        copies[("zy", dy)].wait_recv()
        edges = [(erecv[d, q // 4], R * d + 2 * (q % 4)) for q in range(VX // 2)]
        rows.append(smooth_rows(yrecv[d], edges))
    for q in range(VX // 2):
        pair = smooth_y(z_ref[2 * q], z_ref[2 * q + 1], rows[1][q], rows[0][q])
        y_ref[2 * q], y_ref[2 * q + 1] = pair

    top = math.tanh(4.0)
    strip_rows = 32

    def project(begin, end):
        def strip(s, carry):
            span = pl.ds(pl.multiple_of(s * strip_rows, strip_rows), strip_rows)

            def at(i):
                if i < 0:
                    return rim_ref[i + R, span, :]
                if i >= VX:
                    return rim_ref[i - VX + R, span, :]
                return y_ref[i, span, :]

            total = (R + 1) * at(begin)
            slope = at(begin + R + 1) - at(begin)
            for m in range(1, R + 1):
                low, high = at(begin - m), at(begin + m)
                total = total + (R + 1 - m) * (high + low)
                slope = slope + (high - low)
            for o in range(begin, end):
                proj[o, span, :] = 0.5 + (0.5 / top) * jnp.tanh((8.0 * scale) * total)
                if o < end - 1:
                    total = total + slope
                    if o < end - 2:
                        slope = slope + (at(o + R + 2) - 2.0 * at(o + 1) + at(o - R))
            return carry

        lax.fori_loop(0, VY // strip_rows, strip, 0)
        span = pl.ds(begin, end - begin)
        pltpu.make_async_copy(proj.at[span], out_hbm.at[span], osem.at[0]).start()

    project(R, VX - R)

    for dx, start, slot in sides:
        copies[("x", dx)].wait_recv()
        copies[("zx", dx)].wait_recv()
    for i in range(2 * R):
        zx_ref[i] = smooth_z(xrecv[i], zxrecv[i // R], i % R)
    rows = []
    for d, dy in ends:
        for dx, start, slot in sides:
            copies[("xy", dx, dy)].wait_recv()
            copies[("zxy", dx, dy)].wait_recv()
        edges = [(erecv[d, 4 + q // 4], R * d + 2 * (q % 4)) for q in range(R)]
        rows.append(smooth_rows(yxrecv[d], edges))
    for q in range(R):
        pair = smooth_y(zx_ref[2 * q], zx_ref[2 * q + 1], rows[1][q], rows[0][q])
        rim_ref[2 * q], rim_ref[2 * q + 1] = pair
    project(0, R)
    project(VX - R, VX)

    load_blocks.wait()
    flat = proj.reshape(VX * VY, VZ)
    ones = jnp.ones((8, 128), BF16)
    lanes = (((1,), (1,)), ((), ()))

    def gather(r):
        base = pl.multiple_of(128 * lax.rem(r, 2), 128)
        for j in range(128):
            row = jnp.bitwise_and(blk_s[r, j], VX * VY - 1)
            picked[pl.ds(base + j, 1), :] = flat[pl.ds(row, 1), :]

    def ratio_row(r):
        base = pl.multiple_of(128 * lax.rem(r, 2), 128)
        w = w_recv[pl.ds(r * 8, 8)].reshape(128, 128)
        product = w.astype(F32) * picked[pl.ds(base, 128), :]
        high = product.astype(BF16)
        low = (product - high.astype(F32)).astype(BF16)
        over = lax.dot_general(ones, high, lanes, preferred_element_type=F32)
        over = over + lax.dot_general(ones, low, lanes, preferred_element_type=F32)
        under = lax.dot_general(ones, w, lanes, preferred_element_type=F32)
        ratios[r] = (over / under)[:1]

    def give_back(r, first):
        for i in range(first, 8):
            pltpu.make_async_remote_copy(
                src_ref=ratios.at[r],
                dst_ref=returned.at[me],
                send_sem=rsend.at[0],
                recv_sem=rrecv.at[0],
                device_id=tile_device(lax.rem(me + TILES - 8 * r - i, TILES)),
                device_id_type=MESH,
            ).start()

    def row_step(r, carry):
        give_back(r - 2, 0)
        ratio_row(r - 1)
        gather(r)
        return carry

    rows = TILES // 8
    gather(jnp.int32(0))
    ratio_row(jnp.int32(0))
    gather(jnp.int32(1))
    give_back(jnp.int32(0), 1)
    returned[me] = ratios[0]
    ratio_row(jnp.int32(1))
    gather(jnp.int32(2))
    lax.fori_loop(3, rows, row_step, 0)
    ratio_row(jnp.int32(rows - 1))
    give_back(jnp.int32(rows - 2), 0)
    give_back(jnp.int32(rows - 1), 0)

    offset = jnp.bitwise_and(iota((128, TILES), 1) + (TILES - me), 7)
    chosen = jnp.right_shift(iota((128, TILES), 0), 4) == offset
    live = live_mask(counts_ref[...])
    wait_bytes(returned.at[pl.ds(1, TILES - 1)], rrecv.at[0])
    ratio = jnp.where(chosen, returned[:, 0, :].T, 0.0)
    ratio = jnp.sum(ratio.reshape(8, CAP, TILES), axis=0)
    ratio = jnp.where(live, ratio, 0.0)
    high = ratio.astype(BF16)
    low = (ratio - high.astype(F32)).astype(BF16)
    left = []
    for part in (high, low):
        part = part.astype(F32)
        rows = [jnp.broadcast_to(part[r : r + 1], (16, 128)) for r in range(CAP)]
        left.append(jnp.concatenate(rows, axis=1) * high_ref[...])
    left = jnp.concatenate(left, axis=0).astype(BF16)
    total = lax.dot_general(left, low_ref[...], lanes, preferred_element_type=F32)
    density_ref[...] = total[:16] + total[16:]

    for name in copies:
        copies[name].wait_send()
    wait_bytes(meta_s.at[pl.ds(1, TILES - 1)], msend.at[0])
    wait_bytes(w_recv.at[pl.ds(1, TILES - 1)], wsend.at[0])
    wait_bytes(returned.at[pl.ds(1, TILES - 1)], rsend.at[0])
    wait_bytes(proj, osem.at[0])


def hand_over(in_hbm, out_hbm, held, load_sem, store_sem):
    loads, stores = [], []
    for i in range(PIECES):
        span = pl.ds(i * (VX // PIECES), VX // PIECES)
        loads.append(pltpu.make_async_copy(in_hbm.at[span], held.at[span], load_sem.at[i]))
        stores.append(pltpu.make_async_copy(held.at[span], out_hbm.at[span], store_sem.at[i]))
    for load in loads:
        load.start()
    for load, store in zip(loads, stores):
        load.wait()
        store.start()
    for store in stores:
        store.wait()


VMEM = pl.BlockSpec(memory_space=pltpu.VMEM)
SMEM = pl.BlockSpec(memory_space=pltpu.SMEM)
ANY = pl.BlockSpec(memory_space=pl.ANY)
DMA = pltpu.SemaphoreType.DMA
LIMIT = 60 << 20


def body(
    design,
    forward_edges,
    adjoint_edges,
    edge_basis,
    quad_weights,
    slot_weights,
    slot_elements,
    slot_blocks,
    slot_counts,
):
    shape = jax.ShapeDtypeStruct
    projected, density = pl.pallas_call(
        step_kernel,
        name="density_step",
        out_shape=(shape((VX, VY, VZ), F32), shape((16, 128), F32)),
        in_specs=[ANY, VMEM, VMEM, VMEM, SMEM, VMEM, VMEM, VMEM, VMEM],
        out_specs=(ANY, VMEM),
        scratch_shapes=[
            pltpu.VMEM((VX, VY, VZ), F32),
            pltpu.VMEM((VX, VY, VZ), F32),
            pltpu.VMEM((VX, VY, VZ), BF16),
            pltpu.VMEM((VX, VY, VZ), BF16),
            pltpu.VMEM((2 * R, VY, VZ), BF16),
            pltpu.VMEM((2 * R, VY, VZ), BF16),
            pltpu.VMEM((VX, VY, VZ), F32),
            pltpu.VMEM((2 * R, VY, VZ), F32),
            pltpu.VMEM((VX, VY, VZ), F32),
            pltpu.VMEM((256, 128), F32),
            pltpu.VMEM((TILES, CAP, 128), BF16),
            pltpu.VMEM((TILES, 1, 128), F32),
            pltpu.VMEM((TILES, 1, 128), F32),
            pltpu.VMEM((16, 16, 256), BF16),
            pltpu.VMEM((VY, TILES * CAP), BF16),
            pltpu.VMEM((TILES, CAP, 128), BF16),
            pltpu.VMEM((16, 128), I32),
            pltpu.SMEM((16, 128), I32),
            pltpu.VMEM((TILES // 8, 1, 128), F32),
            pltpu.VMEM((TILES, 1, 128), F32),
            pltpu.VMEM((2, 16, 16, 128), BF16),
            pltpu.VMEM((2, 16, 16, 128), BF16),
            pltpu.VMEM((2, 8, 16, 128), BF16),
            pltpu.VMEM((4, 128, 128), F32),
            pltpu.VMEM((16, TILES * CAP), F32),
            pltpu.VMEM((128, TILES * CAP), BF16),
            pltpu.VMEM((4, 128, 128), BF16),
            pltpu.VMEM((4, 128, 128), BF16),
            pltpu.VMEM((2, 128, 128), BF16),
            pltpu.VMEM((2, 4, R, 128), F32),
            pltpu.VMEM((2, 6, R, 128), F32),
            DMA((1,)),
            DMA((1,)),
            DMA((len(BATCHES),)),
            DMA((1,)),
            DMA((len(BATCHES),)),
            DMA((17,)),
            DMA((17,)),
            DMA((1,)),
            DMA((1,)),
            DMA((1,)),
            DMA((1,)),
        ],
        compiler_params=pltpu.CompilerParams(
            collective_id=1, has_side_effects=True, vmem_limit_bytes=LIMIT
        ),
    )(
        design,
        forward_edges.transpose(1, 0, 2),
        adjoint_edges.transpose(1, 0, 2),
        edge_basis.T,
        quad_weights,
        slot_weights,
        slot_elements.T,
        slot_blocks.T,
        slot_counts,
    )
    projected = pl.pallas_call(
        hand_over,
        name="hand_over",
        out_shape=shape((VX, VY, VZ), F32),
        in_specs=[ANY],
        out_specs=ANY,
        scratch_shapes=[pltpu.VMEM((VX, VY, VZ), F32), DMA((PIECES,)), DMA((PIECES,))],
    )(projected)
    return projected, density.reshape(-1)


def solution(mesh):
    in_specs = (
        P("tx", "ty", "gz"),
        P(None, None, ("tx", "ty", "gz")),
        P(None, None, ("tx", "ty", "gz")),
        P(),
        P(),
        P(("tx", "ty", "gz"), None, None),
        P(("tx", "ty", "gz"), None),
        P(("tx", "ty", "gz"), None),
        P(("tx", "ty", "gz"), None),
    )
    out_specs = (P("tx", "ty", "gz"), P(("tx", "ty", "gz")))
    return jax.shard_map(body, mesh=mesh, in_specs=in_specs, out_specs=out_specs, check_vma=False)
```
